512 devices in a mesh: shot: 16 (over y_hi, x, core), gx: 4 (over y_lo), gy: 8 (over z).
Axes of the slice: x: 4, y: 8 (y_hi: 2, y_lo: 4; y = y_hi * 4 + y_lo), z: 8, core: 2. Of those that a mesh axis runs over, the one named last changes fastest.
Arguments:
- forward_state: bfloat16 [16, 9, 16, 32, 1024], P('shot', None, None, 'gx', 'gy'), may hold values from -6 to 6
- adjoint_state: bfloat16 [16, 9, 16, 32, 1024], P('shot', None, None, 'gx', 'gy'), may hold values from -6 to 6
- lame: float32 [16, 32, 1024], P(None, 'gx', 'gy'), may hold values from 1 to 3
- shear: float32 [16, 32, 1024], P(None, 'gx', 'gy'), may hold values from 0.5 to 1.5
- density: float32 [16, 32, 1024], P(None, 'gx', 'gy'), may hold values from 1 to 2
- wavelet: float32 [16, 3], P('shot'), may hold values from -60 to 60
- residual: float32 [16, 3, 256], P('shot'), may hold values from -60 to 60
- source_x: int32 [16], P('shot'), may hold values from 0 to 31
- source_y: int32 [16], P('shot'), may hold values from 0 to 1023
- receiver_x: int32 [16, 256], P('shot'), may hold values from 0 to 31
- receiver_y: int32 [16, 256], P('shot'), may hold values from 0 to 1023
- aperture: int32 [16, 4, 8], P('shot', 'gx', 'gy'), may hold values 0 or 1
Outputs:
- grad_lambda: float32 [16, 32, 1024], P('shot', 'gx', 'gy')
- grad_mu: float32 [16, 32, 1024], P('shot', 'gx', 'gy')
- grad_rho: float32 [16, 32, 1024], P('shot', 'gx', 'gy')
The draws below stay inside these ranges and needn't reach their ends.
All inputs are finite; a program needn't handle non-finite values. No bound on the sum of `aperture` on one device may be relied on, other than what follows from the above.
Results may differ from the reference program's by a relative error of at most 0.0005.
Values may be sent and summed in bfloat16 or wider, within the bound.
A program may use at most 64 MiB of HBM per device.

```python
import jax
import jax.numpy as jnp
from jax import lax

CX = 8
CY = 128
STEPS = 3
RECEIVERS = 256
FIELDS = 9
SHOTS = 16
GX_TILES = 4
GY_TILES = 8
NX = 32
NY = 1024
NZ = 16


def plant(result, own_key, least, top_value):
    shape = result.shape
    index_at = [jax.random.randint(jax.random.fold_in(own_key, axis), (), 0, shape[axis]) for axis in range(len(shape))]
    result = result.at[tuple(index_at)].set(least)
    longest = shape.index(max(shape))
    index_at[longest] = (index_at[longest] + 1) % shape[longest]
    return result.at[tuple(index_at)].set(top_value)


def steps_of(own_key, extent, cuts, low, top_value):
    def one(dim, parts):
        heights = jax.random.uniform(jax.random.fold_in(jax.random.fold_in(own_key, 6), dim), (parts,), jnp.float32, low / len(cuts), top_value / len(cuts))
        return jnp.repeat(jnp.exp(heights), extent[dim] // parts).reshape((-1,) + (1,) * (len(extent) - dim - 1))

    gain = one(*cuts[0])
    for cut in cuts[1:]:
        gain = gain * one(*cut)
    return gain


def centred(own_key, dims, scale, most, shards=(), kind=jnp.bfloat16):
    loudness = steps_of(own_key, dims, shards, -0.22, 0.18) if shards else 1.0
    result = jax.random.normal(own_key, dims, jnp.float32) * scale * loudness
    return jnp.minimum(jnp.maximum(result, -most), most).astype(kind)


def setup_inputs(seed: int = 0) -> dict:
    splits = jax.random.split(jax.random.key(seed), 13)
    forward_state = centred(splits[0], (SHOTS, FIELDS, NZ, NX, NY), 1.0, 6.0, ((0, 16), (3, 4), (4, 8)))
    adjoint_state = centred(splits[1], (SHOTS, FIELDS, NZ, NX, NY), 1.0, 6.0, ((0, 16), (3, 4), (4, 8)))
    lame = jnp.clip(1.0 + 2.0 * jax.random.uniform(splits[2], (NZ, NX, NY), jnp.float32) ** steps_of(splits[2], (NZ, NX, NY), ((1, 4), (2, 8)), -0.2, 0.2), 1.0, 3.0)
    shear = jnp.clip(0.5 + 1.0 * jax.random.uniform(splits[3], (NZ, NX, NY), jnp.float32) ** steps_of(splits[3], (NZ, NX, NY), ((1, 4), (2, 8)), -0.2, 0.2), 0.5, 1.5)
    density = jnp.clip(1.0 + 1.0 * jax.random.uniform(splits[4], (NZ, NX, NY), jnp.float32) ** steps_of(splits[4], (NZ, NX, NY), ((1, 4), (2, 8)), -0.2, 0.2), 1.0, 2.0)
    wavelet = centred(splits[5], (SHOTS, STEPS), 10.0, 60.0, ((0, 16),), jnp.float32)
    residual = centred(splits[6], (SHOTS, STEPS, RECEIVERS), 10.0, 60.0, ((0, 16),), jnp.float32)
    source_x = plant(jax.random.randint(splits[7], (SHOTS,), 0, NX), jax.random.fold_in(splits[7], 1), 0, NX - 1).astype(jnp.int32)
    source_y = plant(jax.random.randint(splits[8], (SHOTS,), 0, NY), jax.random.fold_in(splits[8], 1), 0, NY - 1).astype(jnp.int32)
    receiver_x = plant(jax.random.randint(splits[9], (SHOTS, RECEIVERS), 0, NX), jax.random.fold_in(splits[9], 1), 0, NX - 1).astype(jnp.int32)
    receiver_y = plant(jax.random.randint(splits[10], (SHOTS, RECEIVERS), 0, NY), jax.random.fold_in(splits[10], 1), 0, NY - 1).astype(jnp.int32)
    aperture = plant((jax.random.randint(splits[11], (SHOTS, GX_TILES, GY_TILES), 0, 4) < 3).astype(jnp.int32), jax.random.fold_in(splits[11], 1), 0, 1)
    return {"forward_state": forward_state, "adjoint_state": adjoint_state, "lame": lame, "shear": shear, "density": density, "wavelet": wavelet, "residual": residual, "source_x": source_x, "source_y": source_y, "receiver_x": receiver_x, "receiver_y": receiver_y, "aperture": aperture}


courant = 0.2


def forward_diff(field, axis):
    size = field.shape[axis]
    tail = lax.slice_in_dim(field, 1, size, axis=axis)
    zero = jnp.zeros_like(lax.slice_in_dim(field, 0, 1, axis=axis))
    return jnp.concatenate([tail, zero], axis=axis) - field


def backward_diff(field, axis):
    size = field.shape[axis]
    head = lax.slice_in_dim(field, 0, size - 1, axis=axis)
    zero = jnp.zeros_like(lax.slice_in_dim(field, 0, 1, axis=axis))
    return field - jnp.concatenate([zero, head], axis=axis)


def velocity_update(velocity, stress, buoyancy):
    factor = courant * buoyancy
    return (velocity[0] + factor * (forward_diff(stress[0], 1) + backward_diff(stress[3], 2) + backward_diff(stress[4], 0)),
            velocity[1] + factor * (backward_diff(stress[3], 1) + forward_diff(stress[1], 2) + backward_diff(stress[5], 0)),
            velocity[2] + factor * (backward_diff(stress[4], 1) + backward_diff(stress[5], 2) + forward_diff(stress[2], 0)))


def strain_parts(velocity):
    return (backward_diff(velocity[0], 1), backward_diff(velocity[1], 2), backward_diff(velocity[2], 0),
            forward_diff(velocity[0], 2) + forward_diff(velocity[1], 1),
            forward_diff(velocity[0], 0) + forward_diff(velocity[2], 1),
            forward_diff(velocity[1], 0) + forward_diff(velocity[2], 2))


def stress_update(stress, strain, lame, shear):
    dilation = strain[0] + strain[1] + strain[2]
    bulk = lame * dilation
    return (stress[0] + courant * (bulk + 2.0 * shear * strain[0]),
            stress[1] + courant * (bulk + 2.0 * shear * strain[1]),
            stress[2] + courant * (bulk + 2.0 * shear * strain[2]),
            stress[3] + courant * shear * strain[3],
            stress[4] + courant * shear * strain[4],
            stress[5] + courant * shear * strain[5])


def image_terms(strain, acceleration, adjoint_strain, adjoint_velocity):
    first = (strain[0] + strain[1] + strain[2]) * (adjoint_strain[0] + adjoint_strain[1] + adjoint_strain[2])
    second = 2.0 * (strain[0] * adjoint_strain[0] + strain[1] * adjoint_strain[1] + strain[2] * adjoint_strain[2])
    second = second + strain[3] * adjoint_strain[3] + strain[4] * adjoint_strain[4] + strain[5] * adjoint_strain[5]
    third = acceleration[0] * adjoint_velocity[0] + acceleration[1] * adjoint_velocity[1] + acceleration[2] * adjoint_velocity[2]
    return (first, second, third)


def one_shot(forward_fields, adjoint_fields, spot_x, spot_y, place_x, place_y, pulse, traces, gate, lame, shear, buoyancy):
    fields = forward_fields.astype(jnp.float32)
    velocity = (fields[0], fields[1], fields[2])
    stress = tuple(fields[index] for index in range(3, 9))
    saved = []
    for step in range(STEPS):
        new_velocity = velocity_update(velocity, stress, buoyancy)
        strain = strain_parts(new_velocity)
        stress = stress_update(stress, strain, lame, shear)
        stress = tuple(stress[index].at[2, spot_x, spot_y].add(pulse[step]) for index in range(3)) + stress[3:]
        acceleration = tuple((new_velocity[index] - velocity[index]) / courant for index in range(3))
        saved.append((strain, acceleration))
        velocity = new_velocity
    fields = adjoint_fields.astype(jnp.float32)
    adjoint_velocity = (fields[0], fields[1], fields[2])
    adjoint_stress = tuple(fields[index] for index in range(3, 9))
    totals = None
    for step in range(STEPS):
        new_velocity = velocity_update(adjoint_velocity, adjoint_stress, buoyancy)
        lifted = new_velocity[2].at[1, place_x, place_y].add(traces[STEPS - 1 - step])
        new_velocity = (new_velocity[0], new_velocity[1], lifted)
        adjoint_strain = strain_parts(new_velocity)
        adjoint_stress = stress_update(adjoint_stress, adjoint_strain, lame, shear)
        strain, acceleration = saved[STEPS - 1 - step]
        terms = jnp.stack(image_terms(strain, acceleration, adjoint_strain, new_velocity))
        totals = terms if totals is None else totals + terms
        adjoint_velocity = new_velocity
    mask = jnp.repeat(jnp.repeat(gate.astype(jnp.float32), CX, axis=0), CY, axis=1)
    return totals * mask[None, None]


def reference(forward_state, adjoint_state, lame, shear, density, wavelet, residual, source_x, source_y, receiver_x, receiver_y, aperture):
    buoyancy = 1.0 / density
    factor = -courant / SHOTS

    def visit(total, item):
        forward_fields, adjoint_fields, spot_x, spot_y, place_x, place_y, pulse, traces, gate = item
        part = one_shot(forward_fields, adjoint_fields, spot_x, spot_y, place_x, place_y, pulse, traces, gate, lame, shear, buoyancy)
        return total + factor * part, None

    start = jnp.zeros((3, NZ, NX, NY), jnp.float32)
    total, _ = lax.scan(visit, start, (forward_state, adjoint_state, source_x, source_y, receiver_x, receiver_y, wavelet, residual, aperture))
    return (total[0], total[1], total[2])
```

```python
import jax
import jax.numpy as jnp
from jax import lax
from jax.experimental import pallas as pl
from jax.experimental.pallas import tpu as pltpu
from jax.sharding import PartitionSpec as P

courant = 0.2
HALO = 3
MESH = pl.DeviceIdType.MESH
CORES, RING, HALVES = 2, 4, 2


def kernel(
    gx_tiles, gy_tiles, steps,
    states, mats, wavelet, source_x, source_y, aperture, residual, receiver_x, receiver_y,
    out_lambda, out_mu, out_rho,
    field, model, x_low, x_high, m_low, m_high, pack, pack_low, pack_high,
    strain, motion, lifted, term, chunks, got_core, sum_core, got_ring, sum_ring, got_half,
    send, recv,
):
    fields2, cx, nz, cy = states.shape
    runs = fields2 // 9
    wide = cx + 2 * HALO
    gx, gy, shot = lax.axis_index("gx"), lax.axis_index("gy"), lax.axis_index("shot")
    half, ring, core = shot // (RING * CORES), lax.rem(shot // CORES, RING), lax.rem(shot, CORES)
    x_start, y_start = gx * cx, gy * cy

    def there(dx, dy):
        ok = None
        for delta, at, count in ((dx, gx, gx_tiles), (dy, gy, gy_tiles)):
            if delta:
                one = at > 0 if delta < 0 else at < count - 1
                ok = one if ok is None else jnp.logical_and(ok, one)
        return ok

    def tile(dx, dy):
        return {"gx": gx + dx, "gy": gy + dy}

    near = [(dx, dy) for dx in (-1, 0, 1) for dy in (-1, 0, 1) if dx or dy]

    def shot_at(h, q, c):
        return {"shot": (h * RING + q) * CORES + c}

    peers = [shot_at(half, ring, 1 - core)]
    peers += [shot_at(half, lax.rem(ring + d, RING), core) for d in range(1, RING)]
    peers += [shot_at(1 - half, ring, core)]

    barrier = pltpu.get_barrier_semaphore()
    for peer in peers:
        pl.semaphore_signal(barrier, inc=1, device_id=peer, device_id_type=MESH)
    for dx, dy in near:
        @pl.when(there(dx, dy))
        def _():
            pl.semaphore_signal(barrier, inc=1, device_id=tile(dx, dy), device_id_type=MESH)

    lane = lax.broadcasted_iota(jnp.int32, (nz, cy), 1)

    def pack_row(x, carry):
        total = jnp.zeros((nz, cy), jnp.float32)
        for f in range(fields2 + 3):
            value = states[f, x].astype(jnp.float32) if f < fields2 else mats[f - fields2, x]
            moved = pltpu.roll(value, 6 * f + 3, axis=1)
            total = jnp.where((lane >= 6 * f) & (lane < 6 * f + 6), moved, total)
        pack[x] = total
        return carry

    lax.fori_loop(0, cx, pack_row, 0)

    along_x = jnp.minimum(gx, 1) + jnp.minimum(gx_tiles - 1 - gx, 1) + 1
    along_y = jnp.minimum(gy, 1) + jnp.minimum(gy_tiles - 1 - gy, 1) + 1
    pl.semaphore_wait(barrier, along_x * along_y - 1 + len(peers))

    def edge(dx):
        return pl.ds(0, HALO) if dx < 0 else pl.ds(cx - HALO, HALO)

    messages = []

    def message(dx, dy, source, target):
        n = len(messages)
        messages.append((dx, dy, pltpu.make_async_remote_copy(
            src_ref=source, dst_ref=target, send_sem=send.at[n], recv_sem=recv.at[n],
            device_id=tile(dx, dy), device_id_type=MESH)))

    for dx in (-1, 1):
        message(dx, 0, mats.at[:, edge(dx)], m_high if dx < 0 else m_low)
    for dx in (-1, 0, 1):
        for dy in (-1, 1):
            side = pack_high if dy < 0 else pack_low
            if dx == 0:
                message(dx, dy, pack, side.at[pl.ds(HALO, cx)])
            else:
                row = HALO + cx if dx < 0 else 0
                message(dx, dy, pack.at[edge(dx)], side.at[pl.ds(row, HALO)])
    shared = len(messages)
    for run in range(runs):
        for dx in (-1, 1):
            side = x_high if dx < 0 else x_low
            message(dx, 0, states.at[pl.ds(9 * run, 9), edge(dx)], side.at[run])
    order = list(range(shared + 2)) + list(range(shared + 2, len(messages)))
    for n in order:
        dx, dy, copy = messages[n]
        @pl.when(there(dx, dy))
        def _():
            copy.start()

    def blank(dx, dy, ref):
        @pl.when(jnp.logical_not(there(dx, dy)))
        def _():
            ref[...] = jnp.zeros(ref.shape, ref.dtype)

    for dx, side, model_side in ((-1, x_low, m_low), (1, x_high, m_high)):
        blank(dx, 0, side)
        blank(dx, 0, model_side)
    for dx in (-1, 0, 1):
        for dy, side in ((-1, pack_low), (1, pack_high)):
            row, count = {-1: (0, HALO), 0: (HALO, cx), 1: (HALO + cx, HALO)}[dx]
            blank(dx, dy, side.at[pl.ds(row, count)])

    def own_row(x, carry):
        for f in range(fields2):
            field[f, x + HALO, :, 0:cy] = states[f, x].astype(jnp.float32)
        for f in range(3):
            model[f, x + HALO, :, 0:cy] = mats[f, x]
        return carry

    lax.fori_loop(0, cx, own_row, 0)

    lanes2 = lax.broadcasted_iota(jnp.int32, (nz, 2 * cy), 1)
    depth = lax.broadcasted_iota(jnp.int32, (nz, 2 * cy), 0)
    column = jnp.where(lanes2 < cy + cy // 2, lanes2, lanes2 - 2 * cy) + y_start

    receivers = receiver_x.shape[1]
    rows = lax.broadcasted_iota(jnp.int32, (16, receivers), 0) + (x_start - HALO)
    hit_x = rows == receiver_x[...]
    cells = lax.broadcasted_iota(jnp.int32, (2 * cy, receivers), 0)
    cells = jnp.where(cells < cy + cy // 2, cells, cells - 2 * cy) + y_start
    hit_y = jnp.where(cells == receiver_y[...], 1.0, 0.0).astype(jnp.float32)
    for n in range(steps):
        picked = jnp.where(hit_x, residual[n : n + 1, :], 0.0)
        lifted[n] = lax.dot_general(
            picked, hit_y, (((1,), (1,)), ((), ())),
            precision=lax.Precision.HIGHEST, preferred_element_type=jnp.float32)

    def wait_recv(n):
        dx, dy, copy = messages[n]
        @pl.when(there(-dx, -dy))
        def _():
            copy.wait_recv()

    lane6 = lax.rem(lane, 6)
    at_edge = (lane < HALO) | (lane >= cy - HALO)

    def unpack_rows():
        def body(x, carry):
            both = jnp.where(lane6 < 3, pack_low[x], pack_high[x])
            for f in range(fields2 + 3):
                moved = pltpu.roll(both, (cy - HALO - 6 * f) % cy, axis=1)
                moved = jnp.where(at_edge, moved, 0.0)
                if f < fields2:
                    field[f, x, :, cy : 2 * cy] = moved
                else:
                    model[f - fields2, x, :, cy : 2 * cy] = moved
            return carry
        lax.fori_loop(0, wide, body, 0)

    def x_halo(run):
        for x in range(HALO):
            def body(f, carry):
                field[9 * run + f, x, :, 0:cy] = x_low[run, f, x].astype(jnp.float32)
                field[9 * run + f, HALO + cx + x, :, 0:cy] = x_high[run, f, x].astype(jnp.float32)
                return carry
            lax.fori_loop(0, 9, body, 0)

    for n in range(shared):
        wait_recv(n)
    for f in range(3):
        for x in range(HALO):
            model[f, x, :, 0:cy] = m_low[f, x]
            model[f, HALO + cx + x, :, 0:cy] = m_high[f, x]
    unpack_rows()

    first_z, last_z = depth == 0, depth == nz - 1

    def y_next(v):
        return pltpu.roll(v, 2 * cy - 1, axis=1)

    def y_back(v):
        return pltpu.roll(v, 1, axis=1)

    def z_next(v):
        return jnp.where(last_z, 0.0, pltpu.roll(v, nz - 1, axis=0))

    def z_back(v):
        return jnp.where(first_z, 0.0, pltpu.roll(v, 1, axis=0))

    pulse_at = jnp.where((depth == 2) & (column == source_y[0]), 1.0, 0.0).astype(jnp.float32)
    lift_at = depth == 1

    for run in range(runs):
        for n in (shared + 2 * run, shared + 2 * run + 1):
            wait_recv(n)
        x_halo(run)
        vx, vy, vz, sxx, syy, szz, sxy, sxz, syz = range(9 * run, 9 * run + 9)
        for n in range(steps):
            def velocity(j, carry):
                k = j + 1
                b0, b1 = model[2, j], model[2, k]
                xy0, xy1, xz0, xz1 = field[sxy, j], field[sxy, k], field[sxz, j], field[sxz, k]
                yy, zz, yz = field[syy, k], field[szz, k], field[syz, k]
                gain_x = b0 * ((field[sxx, k] - field[sxx, j]) + (xy0 - y_back(xy0)) + (xz0 - z_back(xz0)))
                gain_y = b1 * ((xy1 - xy0) + (y_next(yy) - yy) + (yz - z_back(yz)))
                gain_z = b1 * ((xz1 - xz0) + (yz - y_back(yz)) + (z_next(zz) - zz))
                new_x, new_y = field[vx, j] + gain_x, field[vy, k] + gain_y
                new_z = field[vz, k] + gain_z
                if run == 1:
                    row = lifted[steps - 1 - n, pl.ds(k, 1), :]
                    new_z = new_z + jnp.where(lift_at, row, 0.0)
                field[vx, j], field[vy, k], field[vz, k] = new_x, new_y, new_z
                if run == 0:
                    saved = (gain_x * (1.0 / courant), gain_y * (1.0 / courant), gain_z * (1.0 / courant))
                else:
                    saved = (new_x, new_y, new_z)
                motion[run, n, 0, j] = saved[0][:, 0:cy]
                motion[run, n, 1, k] = saved[1][:, 0:cy]
                motion[run, n, 2, k] = saved[2][:, 0:cy]
                return carry

            lax.fori_loop(n, wide - 1 - n, velocity, 0)

            def stress(k, carry):
                x0, y0, z0 = field[vx, k], field[vy, k], field[vz, k]
                e = (
                    x0 - field[vx, k - 1],
                    y0 - y_back(y0),
                    z0 - z_back(z0),
                    (y_next(x0) - x0) + (field[vy, k + 1] - y0),
                    (z_next(x0) - x0) + (field[vz, k + 1] - z0),
                    (z_next(y0) - y0) + (y_next(z0) - z0),
                )
                for c in range(6):
                    strain[run, n, c, k] = e[c][:, 0:cy]
                if n < steps - 1:
                    scaled = courant * model[1, k]
                    bulk = courant * model[0, k] * (e[0] + e[1] + e[2])
                    if run == 0:
                        amount = jnp.where(x_start + k - HALO == source_x[0], wavelet[0, n], 0.0)
                        bulk = bulk + amount * pulse_at
                    for c in range(3):
                        field[sxx + c, k] = field[sxx + c, k] + (bulk + 2.0 * scaled * e[c])
                    for c in range(3, 6):
                        field[sxx + c, k] = field[sxx + c, k] + scaled * e[c]
                return carry

            lax.fori_loop(n + 1, wide - 1 - n, stress, 0)

    factor = (-courant / (HALVES * RING * CORES)) * aperture[0].astype(jnp.float32)

    def image(x, carry):
        k = x + HALO
        first = second = third = jnp.zeros((nz, cy), jnp.float32)
        for m in range(steps):
            n = steps - 1 - m
            e = [strain[0, n, c, k] for c in range(6)]
            f = [strain[1, m, c, k] for c in range(6)]
            first = first + (e[0] + e[1] + e[2]) * (f[0] + f[1] + f[2])
            second = second + 2.0 * (e[0] * f[0] + e[1] * f[1] + e[2] * f[2])
            second = second + e[3] * f[3] + e[4] * f[4] + e[5] * f[5]
            for c in range(3):
                third = third + motion[0, n, c, k] * motion[1, m, c, k]
        term[0, x], term[1, x], term[2, x] = factor * first, factor * second, factor * third
        return carry

    lax.fori_loop(0, cx, image, 0)

    for t in range(3):
        turned = jnp.swapaxes(term[t], 0, 1)
        for z in range(nz):
            chunks[z % CORES, z // (CORES * RING), (z // CORES) % RING, t] = turned[z]

    base = len(messages)
    copy = pltpu.make_async_remote_copy(
        src_ref=chunks.at[1 - core], dst_ref=got_core, send_sem=send.at[base], recv_sem=recv.at[base],
        device_id=peers[0], device_id_type=MESH)
    copy.start()
    copy.wait_recv()
    last = [copy]
    sum_core[...] = chunks[core] + got_core[...]
    rings = []
    for d in range(1, RING):
        copy = pltpu.make_async_remote_copy(
            src_ref=sum_core.at[:, lax.rem(ring + d, RING)], dst_ref=got_ring.at[d - 1],
            send_sem=send.at[base + d], recv_sem=recv.at[base + d],
            device_id=peers[d], device_id_type=MESH)
        copy.start()
        rings.append(copy)
    total = sum_core[:, ring]
    for d in range(1, RING):
        rings[d - 1].wait_recv()
        total = total + got_ring[d - 1]
    sum_ring[...] = total
    copy = pltpu.make_async_remote_copy(
        src_ref=sum_ring.at[1 - half], dst_ref=got_half,
        send_sem=send.at[base + RING], recv_sem=recv.at[base + RING],
        device_id=peers[RING], device_id_type=MESH)
    copy.start()
    copy.wait_recv()
    last += rings + [copy]
    result = sum_ring[half] + got_half[...]
    out_lambda[0], out_mu[0], out_rho[0] = result[0], result[1], result[2]
    for copy in last:
        copy.wait_send()
    for dx, dy, copy in messages:
        @pl.when(there(dx, dy))
        def _():
            copy.wait_send()


def solution(mesh):
    gx_tiles, gy_tiles = mesh.shape["gx"], mesh.shape["gy"]

    def local(
        forward_state, adjoint_state, lame, shear, density, wavelet, residual,
        source_x, source_y, receiver_x, receiver_y, aperture,
    ):
        nz, cx, cy = lame.shape
        steps = wavelet.shape[1]
        wide = cx + 2 * HALO
        states = jnp.concatenate([forward_state[0], adjoint_state[0]]).swapaxes(1, 2)
        mats = jnp.stack([lame, shear, courant * (1.0 / density)]).swapaxes(1, 2)
        f32 = jnp.float32
        out = jax.ShapeDtypeStruct((1, cx, cy), f32)
        vmem = pl.BlockSpec(memory_space=pltpu.VMEM)
        smem = pl.BlockSpec(memory_space=pltpu.SMEM)
        V = pltpu.VMEM
        call = pl.pallas_call(
            lambda *refs: kernel(gx_tiles, gy_tiles, steps, *refs),
            out_shape=(out, out, out),
            in_specs=[vmem, vmem, smem, smem, smem, smem, vmem, vmem, vmem],
            out_specs=(vmem, vmem, vmem),
            scratch_shapes=[
                V((18, wide, nz, 2 * cy), f32),
                V((3, wide, nz, 2 * cy), f32),
                V((2, 9, HALO, nz, cy), jnp.bfloat16),
                V((2, 9, HALO, nz, cy), jnp.bfloat16),
                V((3, HALO, nz, cy), f32),
                V((3, HALO, nz, cy), f32),
                V((cx, nz, cy), f32),
                V((wide, nz, cy), f32),
                V((wide, nz, cy), f32),
                V((2, steps, 6, wide, nz, cy), f32),
                V((2, steps, 3, wide, nz, cy), f32),
                V((steps, 16, 2 * cy), f32),
                V((3, cx, nz, cy), f32),
                V((CORES, HALVES, RING, 3, cx, cy), f32),
                V((HALVES, RING, 3, cx, cy), f32),
                V((HALVES, RING, 3, cx, cy), f32),
                V((RING - 1, HALVES, 3, cx, cy), f32),
                V((HALVES, 3, cx, cy), f32),
                V((3, cx, cy), f32),
                pltpu.SemaphoreType.DMA((17,)),
                pltpu.SemaphoreType.DMA((17,)),
            ],
            compiler_params=pltpu.CompilerParams(collective_id=0, has_side_effects=True),
        )
        return call(
            states, mats, wavelet, source_x, source_y, aperture.reshape(1),
            residual[0], receiver_x, receiver_y,
        )

    return jax.shard_map(
        local,
        mesh=mesh,
        in_specs=(
            P("shot", None, None, "gx", "gy"),
            P("shot", None, None, "gx", "gy"),
            P(None, "gx", "gy"),
            P(None, "gx", "gy"),
            P(None, "gx", "gy"),
            P("shot", None),
            P("shot", None, None),
            P("shot"),
            P("shot"),
            P("shot", None),
            P("shot", None),
            P("shot", "gx", "gy"),
        ),
        out_specs=(P("shot", "gx", "gy"), P("shot", "gx", "gy"), P("shot", "gx", "gy")),
        check_vma=False,
    )
```

```python
import jax
import jax.numpy as jnp
from jax import lax
from jax.experimental import pallas as pl
from jax.experimental.pallas import tpu as pltpu
from jax.sharding import PartitionSpec as P

courant = 0.2
HALO = 3
MESH = pl.DeviceIdType.MESH
CORES, RING, HALVES = 2, 4, 2


def kernel(
    gx_tiles, gy_tiles, steps,
    forward_hbm, adjoint_hbm, lame_hbm, shear_hbm, density_hbm,
    wavelet_hbm, residual_hbm, source_x_hbm, source_y_hbm, receiver_x_hbm, receiver_y_hbm, aperture_hbm,
    out,
    raw, raw_model, wavelet, residual, source_x, source_y, receiver_x, receiver_y, aperture, fetch,
    edge_low, edge_high, edge_model, field, model, x_low, x_high, m_low, m_high, pack, pack_low, pack_high,
    strain, motion, lifted, term, chunks, got_core, sum_core, got_ring, sum_ring, got_half,
    send, recv,
):
    runs, fields, nz, cx, cy = raw.shape
    fields2 = runs * fields
    wide = cx + 2 * HALO
    sources = (
        lame_hbm, shear_hbm, density_hbm, forward_hbm.at[0], adjoint_hbm.at[0], wavelet_hbm, residual_hbm,
        source_x_hbm, source_y_hbm, receiver_x_hbm, receiver_y_hbm, aperture_hbm,
    )
    targets = (
        raw_model.at[0], raw_model.at[1], raw_model.at[2], raw.at[0], raw.at[1], wavelet, residual,
        source_x, source_y, receiver_x, receiver_y, aperture,
    )
    fetched = [
        pltpu.make_async_copy(source, target, fetch.at[n])
        for n, (source, target) in enumerate(zip(sources, targets))
    ]
    for copy in fetched:
        copy.start()

    gx, gy, shot = lax.axis_index("gx"), lax.axis_index("gy"), lax.axis_index("shot")
    half, ring, core = shot // (RING * CORES), lax.rem(shot // CORES, RING), lax.rem(shot, CORES)
    x_start, y_start = gx * cx, gy * cy

    def there(dx, dy):
        ok = None
        for delta, at, count in ((dx, gx, gx_tiles), (dy, gy, gy_tiles)):
            if delta:
                one = at > 0 if delta < 0 else at < count - 1
                ok = one if ok is None else jnp.logical_and(ok, one)
        return ok

    def tile(dx, dy):
        return {"gx": gx + dx, "gy": gy + dy}

    near = [(dx, dy) for dx in (-1, 0, 1) for dy in (-1, 0, 1) if dx or dy]

    def shot_at(h, q, c):
        return {"shot": (h * RING + q) * CORES + c}

    peers = [shot_at(half, ring, 1 - core)]
    peers += [shot_at(half, lax.rem(ring + d, RING), core) for d in range(1, RING)]
    peers += [shot_at(1 - half, ring, core)]

    barrier = pltpu.get_barrier_semaphore()
    for peer in peers:
        pl.semaphore_signal(barrier, inc=1, device_id=peer, device_id_type=MESH)
    for dx, dy in near:
        @pl.when(there(dx, dy))
        def _():
            pl.semaphore_signal(barrier, inc=1, device_id=tile(dx, dy), device_id_type=MESH)

    along_x = jnp.minimum(gx, 1) + jnp.minimum(gx_tiles - 1 - gx, 1) + 1
    along_y = jnp.minimum(gy, 1) + jnp.minimum(gy_tiles - 1 - gy, 1) + 1
    pl.semaphore_wait(barrier, along_x * along_y - 1 + len(peers))

    messages = []

    def message(dx, dy, source, target):
        n = len(messages)
        messages.append((dx, dy, pltpu.make_async_remote_copy(
            src_ref=source, dst_ref=target, send_sem=send.at[n], recv_sem=recv.at[n],
            device_id=tile(dx, dy), device_id_type=MESH)))

    for dx in (-1, 1):
        message(dx, 0, edge_model.at[0 if dx < 0 else 1], m_high if dx < 0 else m_low)
    for dx in (-1, 0, 1):
        for dy in (-1, 1):
            side = pack_high if dy < 0 else pack_low
            if dx == 0:
                message(dx, dy, pack, side.at[pl.ds(HALO, cx)])
            else:
                row = HALO + cx if dx < 0 else 0
                source = pack.at[pl.ds(0 if dx < 0 else cx - HALO, HALO)]
                message(dx, dy, source, side.at[pl.ds(row, HALO)])
    shared = len(messages)
    for run in range(runs):
        for dx in (-1, 1):
            side = x_high if dx < 0 else x_low
            message(dx, 0, (edge_low if dx < 0 else edge_high).at[run], side.at[run])

    def issue(numbers):
        for n in numbers:
            dx, dy, copy = messages[n]
            @pl.when(there(dx, dy))
            def _():
                copy.start()

    for n in range(3):
        fetched[n].wait()
    for f in range(3):
        value = raw_model[f]
        if f == 2:
            value = courant * (1.0 / value)
        turned = jnp.swapaxes(value, 0, 1)
        model[f, HALO : HALO + cx, :, 0:cy] = turned
        edge_model[0, f] = turned[:HALO]
        edge_model[1, f] = turned[cx - HALO :]
    issue((0, 1))
    for run in range(runs):
        fetched[3 + run].wait()

        def turn(f, carry):
            turned = jnp.swapaxes(raw[run, f].astype(jnp.float32), 0, 1)
            field[fields * run + f, HALO : HALO + cx, :, 0:cy] = turned
            edge_low[run, f] = turned[:HALO].astype(jnp.bfloat16)
            edge_high[run, f] = turned[cx - HALO :].astype(jnp.bfloat16)
            return carry

        lax.fori_loop(0, fields, turn, 0)
        if run == 0:
            issue((shared, shared + 1))

    lane = lax.broadcasted_iota(jnp.int32, (nz, cy), 1)

    def pack_row(x, carry):
        total = jnp.zeros((nz, cy), jnp.float32)
        for f in range(fields2 + 3):
            value = (field[f, x + HALO] if f < fields2 else model[f - fields2, x + HALO])[:, 0:cy]
            moved = pltpu.roll(value, 6 * f + 3, axis=1)
            total = jnp.where((lane >= 6 * f) & (lane < 6 * f + 6), moved, total)
        pack[x] = total
        return carry

    lax.fori_loop(0, cx, pack_row, 0)
    issue(range(2, shared))

    def blank(dx, dy, ref):
        @pl.when(jnp.logical_not(there(dx, dy)))
        def _():
            ref[...] = jnp.zeros(ref.shape, ref.dtype)

    for dx, side, model_side in ((-1, x_low, m_low), (1, x_high, m_high)):
        blank(dx, 0, side)
        blank(dx, 0, model_side)
    for dx in (-1, 0, 1):
        for dy, side in ((-1, pack_low), (1, pack_high)):
            row, count = {-1: (0, HALO), 0: (HALO, cx), 1: (HALO + cx, HALO)}[dx]
            blank(dx, dy, side.at[pl.ds(row, count)])

    for copy in fetched[5:]:
        copy.wait()

    lanes2 = lax.broadcasted_iota(jnp.int32, (nz, 2 * cy), 1)
    depth = lax.broadcasted_iota(jnp.int32, (nz, 2 * cy), 0)
    column = jnp.where(lanes2 < cy + cy // 2, lanes2, lanes2 - 2 * cy) + y_start

    receivers = receiver_x.shape[1]
    rows = lax.broadcasted_iota(jnp.int32, (16, receivers), 0) + (x_start - HALO)
    hit_x = rows == receiver_x[...]
    cells = lax.broadcasted_iota(jnp.int32, (2 * cy, receivers), 0)
    cells = jnp.where(cells < cy + cy // 2, cells, cells - 2 * cy) + y_start
    hit_y = jnp.where(cells == receiver_y[...], 1.0, 0.0).astype(jnp.float32)
    for n in range(steps):
        picked = jnp.where(hit_x, residual[n], 0.0)
        lifted[n] = lax.dot_general(
            picked, hit_y, (((1,), (1,)), ((), ())),
            precision=lax.Precision.HIGHEST, preferred_element_type=jnp.float32)

    def wait_recv(n):
        dx, dy, copy = messages[n]
        @pl.when(there(-dx, -dy))
        def _():
            copy.wait_recv()

    lane6 = lax.rem(lane, 6)
    at_edge = (lane < HALO) | (lane >= cy - HALO)

    def unpack_rows():
        def body(x, carry):
            both = jnp.where(lane6 < 3, pack_low[x], pack_high[x])
            for f in range(fields2 + 3):
                moved = pltpu.roll(both, (cy - HALO - 6 * f) % cy, axis=1)
                moved = jnp.where(at_edge, moved, 0.0)
                if f < fields2:
                    field[f, x, :, cy : 2 * cy] = moved
                else:
                    model[f - fields2, x, :, cy : 2 * cy] = moved
            return carry
        lax.fori_loop(0, wide, body, 0)

    def x_halo(run):
        for x in range(HALO):
            def body(f, carry):
                field[9 * run + f, x, :, 0:cy] = x_low[run, f, x].astype(jnp.float32)
                field[9 * run + f, HALO + cx + x, :, 0:cy] = x_high[run, f, x].astype(jnp.float32)
                return carry
            lax.fori_loop(0, 9, body, 0)

    for n in range(shared + 2):
        wait_recv(n)
    for f in range(3):
        for x in range(HALO):
            model[f, x, :, 0:cy] = m_low[f, x]
            model[f, HALO + cx + x, :, 0:cy] = m_high[f, x]
    issue(range(shared + 2, len(messages)))
    unpack_rows()

    first_z, last_z = depth == 0, depth == nz - 1

    def y_next(v):
        return pltpu.roll(v, 2 * cy - 1, axis=1)

    def y_back(v):
        return pltpu.roll(v, 1, axis=1)

    def z_next(v):
        return jnp.where(last_z, 0.0, pltpu.roll(v, nz - 1, axis=0))

    def z_back(v):
        return jnp.where(first_z, 0.0, pltpu.roll(v, 1, axis=0))

    pulse_at = jnp.where((depth == 2) & (column == source_y[0]), 1.0, 0.0).astype(jnp.float32)
    lift_at = depth == 1

    for run in range(runs):
        if run == 1:
            for n in (shared + 2, shared + 3):
                wait_recv(n)
        x_halo(run)
        vx, vy, vz, sxx, syy, szz, sxy, sxz, syz = range(9 * run, 9 * run + 9)
        for n in range(steps):
            def velocity(j, carry):
                k = j + 1
                b0, b1 = model[2, j], model[2, k]
                xy0, xy1, xz0, xz1 = field[sxy, j], field[sxy, k], field[sxz, j], field[sxz, k]
                yy, zz, yz = field[syy, k], field[szz, k], field[syz, k]
                gain_x = b0 * ((field[sxx, k] - field[sxx, j]) + (xy0 - y_back(xy0)) + (xz0 - z_back(xz0)))
                gain_y = b1 * ((xy1 - xy0) + (y_next(yy) - yy) + (yz - z_back(yz)))
                gain_z = b1 * ((xz1 - xz0) + (yz - y_back(yz)) + (z_next(zz) - zz))
                new_x, new_y = field[vx, j] + gain_x, field[vy, k] + gain_y
                new_z = field[vz, k] + gain_z
                if run == 1:
                    row = lifted[steps - 1 - n, pl.ds(k, 1), :]
                    new_z = new_z + jnp.where(lift_at, row, 0.0)
                field[vx, j], field[vy, k], field[vz, k] = new_x, new_y, new_z
                if run == 0:
                    saved = (gain_x * (1.0 / courant), gain_y * (1.0 / courant), gain_z * (1.0 / courant))
                else:
                    saved = (new_x, new_y, new_z)
                motion[run, n, 0, j] = saved[0][:, 0:cy]
                motion[run, n, 1, k] = saved[1][:, 0:cy]
                motion[run, n, 2, k] = saved[2][:, 0:cy]
                return carry

            lax.fori_loop(n, wide - 1 - n, velocity, 0)

            def stress(k, carry):
                x0, y0, z0 = field[vx, k], field[vy, k], field[vz, k]
                e = (
                    x0 - field[vx, k - 1],
                    y0 - y_back(y0),
                    z0 - z_back(z0),
                    (y_next(x0) - x0) + (field[vy, k + 1] - y0),
                    (z_next(x0) - x0) + (field[vz, k + 1] - z0),
                    (z_next(y0) - y0) + (y_next(z0) - z0),
                )
                for c in range(6):
                    strain[run, n, c, k] = e[c][:, 0:cy]
                if n < steps - 1:
                    scaled = courant * model[1, k]
                    bulk = courant * model[0, k] * (e[0] + e[1] + e[2])
                    if run == 0:
                        amount = jnp.where(x_start + k - HALO == source_x[0], wavelet[0, n], 0.0)
                        bulk = bulk + amount * pulse_at
                    for c in range(3):
                        field[sxx + c, k] = field[sxx + c, k] + (bulk + 2.0 * scaled * e[c])
                    for c in range(3, 6):
                        field[sxx + c, k] = field[sxx + c, k] + scaled * e[c]
                return carry

            lax.fori_loop(n + 1, wide - 1 - n, stress, 0)

    factor = (-courant / (HALVES * RING * CORES)) * aperture[0, 0, 0].astype(jnp.float32)

    def image(x, carry):
        k = x + HALO
        first = second = third = jnp.zeros((nz, cy), jnp.float32)
        for m in range(steps):
            n = steps - 1 - m
            e = [strain[0, n, c, k] for c in range(6)]
            f = [strain[1, m, c, k] for c in range(6)]
            first = first + (e[0] + e[1] + e[2]) * (f[0] + f[1] + f[2])
            second = second + 2.0 * (e[0] * f[0] + e[1] * f[1] + e[2] * f[2])
            second = second + e[3] * f[3] + e[4] * f[4] + e[5] * f[5]
            for c in range(3):
                third = third + motion[0, n, c, k] * motion[1, m, c, k]
        term[0, x], term[1, x], term[2, x] = factor * first, factor * second, factor * third
        return carry

    lax.fori_loop(0, cx, image, 0)

    for t in range(3):
        turned = jnp.swapaxes(term[t], 0, 1)
        for z in range(nz):
            chunks[z % CORES, z // (CORES * RING), (z // CORES) % RING, t] = turned[z]

    base = len(messages)
    copy = pltpu.make_async_remote_copy(
        src_ref=chunks.at[1 - core], dst_ref=got_core, send_sem=send.at[base], recv_sem=recv.at[base],
        device_id=peers[0], device_id_type=MESH)
    copy.start()
    copy.wait_recv()
    last = [copy]
    sum_core[...] = chunks[core] + got_core[...]
    rings = []
    for d in range(1, RING):
        copy = pltpu.make_async_remote_copy(
            src_ref=sum_core.at[:, lax.rem(ring + d, RING)], dst_ref=got_ring.at[d - 1],
            send_sem=send.at[base + d], recv_sem=recv.at[base + d],
            device_id=peers[d], device_id_type=MESH)
        copy.start()
        rings.append(copy)
    total = sum_core[:, ring]
    for d in range(1, RING):
        rings[d - 1].wait_recv()
        total = total + got_ring[d - 1]
    sum_ring[...] = total
    copy = pltpu.make_async_remote_copy(
        src_ref=sum_ring.at[1 - half], dst_ref=got_half,
        send_sem=send.at[base + RING], recv_sem=recv.at[base + RING],
        device_id=peers[RING], device_id_type=MESH)
    copy.start()
    copy.wait_recv()
    last += rings + [copy]
    result = sum_ring[half] + got_half[...]
    out[...] = result
    for copy in last:
        copy.wait_send()
    for dx, dy, copy in messages:
        @pl.when(there(dx, dy))
        def _():
            copy.wait_send()


def solution(mesh):
    gx_tiles, gy_tiles = mesh.shape["gx"], mesh.shape["gy"]

    def local(
        forward_state, adjoint_state, lame, shear, density, wavelet, residual,
        source_x, source_y, receiver_x, receiver_y, aperture,
    ):
        nz, cx, cy = lame.shape
        steps = wavelet.shape[1]
        wide = cx + 2 * HALO
        f32 = jnp.float32
        out = jax.ShapeDtypeStruct((3, cx, cy), f32)
        vmem = pl.BlockSpec(memory_space=pltpu.VMEM)
        anywhere = pl.BlockSpec(memory_space=pl.ANY)
        S = pltpu.SMEM
        V = pltpu.VMEM
        call = pl.pallas_call(
            lambda *refs: kernel(gx_tiles, gy_tiles, steps, *refs),
            out_shape=out,
            in_specs=[anywhere] * 12,
            out_specs=vmem,
            scratch_shapes=[
                V((2, 9, nz, cx, cy), jnp.bfloat16),
                V((3, nz, cx, cy), f32),
                S((1, steps), f32),
                V((steps, 1, residual.shape[2]), f32),
                S((1,), jnp.int32),
                S((1,), jnp.int32),
                V((1, residual.shape[2]), jnp.int32),
                V((1, residual.shape[2]), jnp.int32),
                S((1, 1, 1), jnp.int32),
                pltpu.SemaphoreType.DMA((12,)),
                V((2, 9, HALO, nz, cy), jnp.bfloat16),
                V((2, 9, HALO, nz, cy), jnp.bfloat16),
                V((2, 3, HALO, nz, cy), f32),
                V((18, wide, nz, 2 * cy), f32),
                V((3, wide, nz, 2 * cy), f32),
                V((2, 9, HALO, nz, cy), jnp.bfloat16),
                V((2, 9, HALO, nz, cy), jnp.bfloat16),
                V((3, HALO, nz, cy), f32),
                V((3, HALO, nz, cy), f32),
                V((cx, nz, cy), f32),
                V((wide, nz, cy), f32),
                V((wide, nz, cy), f32),
                V((2, steps, 6, wide, nz, cy), f32),
                V((2, steps, 3, wide, nz, cy), f32),
                V((steps, 16, 2 * cy), f32),
                V((3, cx, nz, cy), f32),
                V((CORES, HALVES, RING, 3, cx, cy), f32),
                V((HALVES, RING, 3, cx, cy), f32),
                V((HALVES, RING, 3, cx, cy), f32),
                V((RING - 1, HALVES, 3, cx, cy), f32),
                V((HALVES, 3, cx, cy), f32),
                V((3, cx, cy), f32),
                pltpu.SemaphoreType.DMA((17,)),
                pltpu.SemaphoreType.DMA((17,)),
            ],
            compiler_params=pltpu.CompilerParams(collective_id=0, has_side_effects=True),
        )
        sums = call(
            forward_state, adjoint_state, lame, shear, density, wavelet, residual.swapaxes(0, 1),
            source_x, source_y, receiver_x, receiver_y, aperture,
        )
        return sums[0:1], sums[1:2], sums[2:3]

    return jax.shard_map(
        local,
        mesh=mesh,
        in_specs=(
            P("shot", None, None, "gx", "gy"),
            P("shot", None, None, "gx", "gy"),
            P(None, "gx", "gy"),
            P(None, "gx", "gy"),
            P(None, "gx", "gy"),
            P("shot", None),
            P("shot", None, None),
            P("shot"),
            P("shot"),
            P("shot", None),
            P("shot", None),
            P("shot", "gx", "gy"),
        ),
        out_specs=(P("shot", "gx", "gy"), P("shot", "gx", "gy"), P("shot", "gx", "gy")),
        check_vma=False,
    )
```

```python
import jax
import jax.numpy as jnp
from jax import lax
from jax.experimental import pallas as pl
from jax.experimental.pallas import tpu as pltpu
from jax.sharding import PartitionSpec as P

courant = 0.2
HALO = 3
MESH = pl.DeviceIdType.MESH
CORES, RING, HALVES = 2, 4, 2


def kernel(
    gx_tiles, gy_tiles, steps,
    forward_hbm, adjoint_hbm, lame_hbm, shear_hbm, density_hbm,
    wavelet_hbm, residual_hbm, source_x_hbm, source_y_hbm, receiver_x_hbm, receiver_y_hbm, aperture_hbm,
    out,
    raw, raw_model, wavelet, residual, source_x, source_y, receiver_x, receiver_y, aperture, fetch,
    edge_low, edge_high, edge_model, field, model, x_low, x_high, m_low, m_high, pack, pack_low, pack_high,
    strain, motion, lifted, term, chunks, got_core, sum_core, got_ring, sum_ring, got_half,
    send, recv,
):
    runs, fields, nz, cx, cy = raw.shape
    fields2 = runs * fields
    wide = cx + 2 * HALO
    sources = (
        lame_hbm, shear_hbm, density_hbm, forward_hbm.at[0], adjoint_hbm.at[0], wavelet_hbm, residual_hbm,
        source_x_hbm, source_y_hbm, receiver_x_hbm, receiver_y_hbm, aperture_hbm,
    )
    targets = (
        raw_model.at[0], raw_model.at[1], raw_model.at[2], raw.at[0], raw.at[1], wavelet, residual,
        source_x, source_y, receiver_x, receiver_y, aperture,
    )
    fetched = [
        pltpu.make_async_copy(source, target, fetch.at[n])
        for n, (source, target) in enumerate(zip(sources, targets))
    ]
    for copy in fetched:
        copy.start()

    gx, gy, shot = lax.axis_index("gx"), lax.axis_index("gy"), lax.axis_index("shot")
    half, ring, core = shot // (RING * CORES), lax.rem(shot // CORES, RING), lax.rem(shot, CORES)
    x_start, y_start = gx * cx, gy * cy

    def there(dx, dy):
        ok = None
        for delta, at, count in ((dx, gx, gx_tiles), (dy, gy, gy_tiles)):
            if delta:
                one = at > 0 if delta < 0 else at < count - 1
                ok = one if ok is None else jnp.logical_and(ok, one)
        return ok

    def tile(dx, dy):
        return {"gx": gx + dx, "gy": gy + dy}

    near = [(dx, dy) for dx in (-1, 0, 1) for dy in (-1, 0, 1) if dx or dy]

    def shot_at(h, q, c):
        return {"shot": (h * RING + q) * CORES + c}

    peers = [shot_at(half, ring, 1 - core)]
    peers += [shot_at(half, lax.rem(ring + d, RING), core) for d in range(1, RING)]
    peers += [shot_at(1 - half, ring, core)]

    barrier = pltpu.get_barrier_semaphore()
    for peer in peers:
        pl.semaphore_signal(barrier, inc=1, device_id=peer, device_id_type=MESH)
    for dx, dy in near:
        @pl.when(there(dx, dy))
        def _():
            pl.semaphore_signal(barrier, inc=1, device_id=tile(dx, dy), device_id_type=MESH)

    along_x = jnp.minimum(gx, 1) + jnp.minimum(gx_tiles - 1 - gx, 1) + 1
    along_y = jnp.minimum(gy, 1) + jnp.minimum(gy_tiles - 1 - gy, 1) + 1
    pl.semaphore_wait(barrier, along_x * along_y - 1 + len(peers))

    messages = []

    def message(dx, dy, source, target):
        n = len(messages)
        messages.append((dx, dy, pltpu.make_async_remote_copy(
            src_ref=source, dst_ref=target, send_sem=send.at[n], recv_sem=recv.at[n],
            device_id=tile(dx, dy), device_id_type=MESH)))

    for dx in (-1, 1):
        message(dx, 0, edge_model.at[0 if dx < 0 else 1], m_high if dx < 0 else m_low)
    for dx in (-1, 0, 1):
        for dy in (-1, 1):
            side = pack_high if dy < 0 else pack_low
            if dx == 0:
                message(dx, dy, pack, side.at[pl.ds(HALO, cx)])
            else:
                row = HALO + cx if dx < 0 else 0
                source = pack.at[pl.ds(0 if dx < 0 else cx - HALO, HALO)]
                message(dx, dy, source, side.at[pl.ds(row, HALO)])
    shared = len(messages)
    for run in range(runs):
        for dx in (-1, 1):
            side = x_high if dx < 0 else x_low
            message(dx, 0, (edge_low if dx < 0 else edge_high).at[run], side.at[run])

    def issue(numbers):
        for n in numbers:
            dx, dy, copy = messages[n]
            @pl.when(there(dx, dy))
            def _():
                copy.start()

    for n in range(3):
        fetched[n].wait()
    for f in range(3):
        value = raw_model[f]
        if f == 2:
            value = courant * (1.0 / value)
        turned = jnp.swapaxes(value, 0, 1)
        model[f, HALO : HALO + cx, :, 0:cy] = turned
        edge_model[0, f] = turned[:HALO]
        edge_model[1, f] = turned[cx - HALO :]
    issue((0, 1))
    for run in range(runs):
        fetched[3 + run].wait()

        def turn(f, carry):
            turned = jnp.swapaxes(raw[run, f].astype(jnp.float32), 0, 1)
            field[fields * run + f, HALO : HALO + cx, :, 0:cy] = turned
            edge_low[run, f] = turned[:HALO].astype(jnp.bfloat16)
            edge_high[run, f] = turned[cx - HALO :].astype(jnp.bfloat16)
            return carry

        lax.fori_loop(0, fields, turn, 0)
        if run == 0:
            issue((shared, shared + 1))

    lane = lax.broadcasted_iota(jnp.int32, (nz, cy), 1)

    def pack_row(x, carry):
        total = jnp.zeros((nz, cy), jnp.float32)
        for f in range(fields2 + 3):
            value = (field[f, x + HALO] if f < fields2 else model[f - fields2, x + HALO])[:, 0:cy]
            moved = pltpu.roll(value, 6 * f + 3, axis=1)
            total = jnp.where((lane >= 6 * f) & (lane < 6 * f + 6), moved, total)
        pack[x] = total
        return carry

    lax.fori_loop(0, cx, pack_row, 0)
    issue((4, 5, 2, 3, 6, 7, shared + 2, shared + 3))

    def blank(dx, dy, ref):
        @pl.when(jnp.logical_not(there(dx, dy)))
        def _():
            ref[...] = jnp.zeros(ref.shape, ref.dtype)

    for dx, side, model_side in ((-1, x_low, m_low), (1, x_high, m_high)):
        blank(dx, 0, side)
        blank(dx, 0, model_side)
    for dx in (-1, 0, 1):
        for dy, side in ((-1, pack_low), (1, pack_high)):
            row, count = {-1: (0, HALO), 0: (HALO, cx), 1: (HALO + cx, HALO)}[dx]
            blank(dx, dy, side.at[pl.ds(row, count)])

    for copy in fetched[5:]:
        copy.wait()

    lanes2 = lax.broadcasted_iota(jnp.int32, (nz, 2 * cy), 1)
    depth = lax.broadcasted_iota(jnp.int32, (nz, 2 * cy), 0)
    column = jnp.where(lanes2 < cy + cy // 2, lanes2, lanes2 - 2 * cy) + y_start

    receivers = receiver_x.shape[1]
    rows = lax.broadcasted_iota(jnp.int32, (16, receivers), 0) + (x_start - HALO)
    hit_x = rows == receiver_x[...]
    cells = lax.broadcasted_iota(jnp.int32, (2 * cy, receivers), 0)
    cells = jnp.where(cells < cy + cy // 2, cells, cells - 2 * cy) + y_start
    hit_y = jnp.where(cells == receiver_y[...], 1.0, 0.0).astype(jnp.float32)
    for n in range(steps):
        picked = jnp.where(hit_x, residual[n], 0.0)
        lifted[n] = lax.dot_general(
            picked, hit_y, (((1,), (1,)), ((), ())),
            precision=lax.Precision.HIGHEST, preferred_element_type=jnp.float32)

    def wait_recv(n):
        dx, dy, copy = messages[n]
        @pl.when(there(-dx, -dy))
        def _():
            copy.wait_recv()

    lane6 = lax.rem(lane, 6)
    at_edge = (lane < HALO) | (lane >= cy - HALO)

    def unpack_row(x):
        both = jnp.where(lane6 < 3, pack_low[x], pack_high[x])
        for f in range(fields2 + 3):
            moved = pltpu.roll(both, (cy - HALO - 6 * f) % cy, axis=1)
            moved = jnp.where(at_edge, moved, 0.0)
            if f < fields2:
                field[f, x, :, cy : 2 * cy] = moved
            else:
                model[f - fields2, x, :, cy : 2 * cy] = moved

    def loop(low, high, *bodies):
        def body(i, carry):
            for one in bodies:
                one(i)
            return carry
        lax.fori_loop(low, high, body, 0)

    def x_halo(run):
        def body(f):
            for x in range(HALO):
                field[9 * run + f, x, :, 0:cy] = x_low[run, f, x].astype(jnp.float32)
                field[9 * run + f, HALO + cx + x, :, 0:cy] = x_high[run, f, x].astype(jnp.float32)
        loop(0, 9, body)

    first_z, last_z = depth == 0, depth == nz - 1

    def y_next(v):
        return pltpu.roll(v, 2 * cy - 1, axis=1)

    def y_back(v):
        return pltpu.roll(v, 1, axis=1)

    def z_next(v):
        return jnp.where(last_z, 0.0, pltpu.roll(v, nz - 1, axis=0))

    def z_back(v):
        return jnp.where(first_z, 0.0, pltpu.roll(v, 1, axis=0))

    pulse_at = jnp.where((depth == 2) & (column == source_y[0]), 1.0, 0.0).astype(jnp.float32)
    lift_at = depth == 1

    def velocity(run, n, j):
        vx, vy, vz, sxx, syy, szz, sxy, sxz, syz = range(9 * run, 9 * run + 9)
        k = j + 1
        b0, b1 = model[2, j], model[2, k]
        xy0, xy1, xz0, xz1 = field[sxy, j], field[sxy, k], field[sxz, j], field[sxz, k]
        yy, zz, yz = field[syy, k], field[szz, k], field[syz, k]
        gain_x = b0 * ((field[sxx, k] - field[sxx, j]) + (xy0 - y_back(xy0)) + (xz0 - z_back(xz0)))
        gain_y = b1 * ((xy1 - xy0) + (y_next(yy) - yy) + (yz - z_back(yz)))
        gain_z = b1 * ((xz1 - xz0) + (yz - y_back(yz)) + (z_next(zz) - zz))
        new_x, new_y = field[vx, j] + gain_x, field[vy, k] + gain_y
        new_z = field[vz, k] + gain_z
        if run == 1:
            row = lifted[steps - 1 - n, pl.ds(k, 1), :]
            new_z = new_z + jnp.where(lift_at, row, 0.0)
        field[vx, j], field[vy, k], field[vz, k] = new_x, new_y, new_z
        if run == 0:
            saved = (gain_x * (1.0 / courant), gain_y * (1.0 / courant), gain_z * (1.0 / courant))
        else:
            saved = (new_x, new_y, new_z)
        motion[run, n, 0, j] = saved[0][:, 0:cy]
        motion[run, n, 1, k] = saved[1][:, 0:cy]
        motion[run, n, 2, k] = saved[2][:, 0:cy]

    def stress(run, n, k):
        vx, vy, vz, sxx, syy, szz, sxy, sxz, syz = range(9 * run, 9 * run + 9)
        x0, y0, z0 = field[vx, k], field[vy, k], field[vz, k]
        e = (
            x0 - field[vx, k - 1],
            y0 - y_back(y0),
            z0 - z_back(z0),
            (y_next(x0) - x0) + (field[vy, k + 1] - y0),
            (z_next(x0) - x0) + (field[vz, k + 1] - z0),
            (z_next(y0) - y0) + (y_next(z0) - z0),
        )
        for c in range(6):
            strain[run, n, c, k] = e[c][:, 0:cy]
        if n < steps - 1:
            scaled = courant * model[1, k]
            bulk = courant * model[0, k] * (e[0] + e[1] + e[2])
            if run == 0:
                amount = jnp.where(x_start + k - HALO == source_x[0], wavelet[0, n], 0.0)
                bulk = bulk + amount * pulse_at
            for c in range(3):
                field[sxx + c, k] = field[sxx + c, k] + (bulk + 2.0 * scaled * e[c])
            for c in range(3, 6):
                field[sxx + c, k] = field[sxx + c, k] + scaled * e[c]

    wait_recv(4)
    wait_recv(5)
    loop(0, cx, lambda x: unpack_row(x + HALO))
    for n in range(steps):
        loop(HALO + n, cx + HALO - 1 - n, lambda j: velocity(0, n, j), lambda j: velocity(1, n, j))
        loop(HALO + 1 + n, cx + HALO - 1 - n, lambda k: stress(0, n, k), lambda k: stress(1, n, k))

    for n in (0, 1, 2, 3, 6, 7):
        wait_recv(n)
    for f in range(3):
        for x in range(HALO):
            model[f, x, :, 0:cy] = m_low[f, x]
            model[f, HALO + cx + x, :, 0:cy] = m_high[f, x]
    loop(0, HALO, unpack_row, lambda x: unpack_row(x + HALO + cx))
    for run in range(runs):
        wait_recv(shared + 2 * run)
        wait_recv(shared + 2 * run + 1)
        x_halo(run)
        for n in range(steps):
            high = cx + HALO - 1 - n
            loop(0, HALO, lambda i: velocity(run, n, i + n), lambda i: velocity(run, n, i + high))
            loop(0, HALO, lambda i: stress(run, n, i + n + 1), lambda i: stress(run, n, i + high))

    factor = (-courant / (HALVES * RING * CORES)) * aperture[0, 0, 0].astype(jnp.float32)

    def image(x, carry):
        k = x + HALO
        first = second = third = jnp.zeros((nz, cy), jnp.float32)
        for m in range(steps):
            n = steps - 1 - m
            e = [strain[0, n, c, k] for c in range(6)]
            f = [strain[1, m, c, k] for c in range(6)]
            first = first + (e[0] + e[1] + e[2]) * (f[0] + f[1] + f[2])
            second = second + 2.0 * (e[0] * f[0] + e[1] * f[1] + e[2] * f[2])
            second = second + e[3] * f[3] + e[4] * f[4] + e[5] * f[5]
            for c in range(3):
                third = third + motion[0, n, c, k] * motion[1, m, c, k]
        term[0, x], term[1, x], term[2, x] = factor * first, factor * second, factor * third
        return carry

    lax.fori_loop(0, cx, image, 0)

    for t in range(3):
        turned = jnp.swapaxes(term[t], 0, 1)
        for z in range(nz):
            chunks[z % CORES, z // (CORES * RING), (z // CORES) % RING, t] = turned[z]

    base = len(messages)
    copy = pltpu.make_async_remote_copy(
        src_ref=chunks.at[1 - core], dst_ref=got_core, send_sem=send.at[base], recv_sem=recv.at[base],
        device_id=peers[0], device_id_type=MESH)
    copy.start()
    copy.wait_recv()
    last = [copy]
    sum_core[...] = chunks[core] + got_core[...]
    rings = []
    for d in range(1, RING):
        copy = pltpu.make_async_remote_copy(
            src_ref=sum_core.at[:, lax.rem(ring + d, RING)], dst_ref=got_ring.at[d - 1],
            send_sem=send.at[base + d], recv_sem=recv.at[base + d],
            device_id=peers[d], device_id_type=MESH)
        copy.start()
        rings.append(copy)
    total = sum_core[:, ring]
    for d in range(1, RING):
        rings[d - 1].wait_recv()
        total = total + got_ring[d - 1]
    sum_ring[...] = total
    copy = pltpu.make_async_remote_copy(
        src_ref=sum_ring.at[1 - half], dst_ref=got_half,
        send_sem=send.at[base + RING], recv_sem=recv.at[base + RING],
        device_id=peers[RING], device_id_type=MESH)
    copy.start()
    copy.wait_recv()
    last += rings + [copy]
    result = sum_ring[half] + got_half[...]
    out[...] = result
    for copy in last:
        copy.wait_send()
    for dx, dy, copy in messages:
        @pl.when(there(dx, dy))
        def _():
            copy.wait_send()


def solution(mesh):
    gx_tiles, gy_tiles = mesh.shape["gx"], mesh.shape["gy"]

    def local(
        forward_state, adjoint_state, lame, shear, density, wavelet, residual,
        source_x, source_y, receiver_x, receiver_y, aperture,
    ):
        nz, cx, cy = lame.shape
        steps = wavelet.shape[1]
        wide = cx + 2 * HALO
        f32 = jnp.float32
        out = jax.ShapeDtypeStruct((3, cx, cy), f32)
        vmem = pl.BlockSpec(memory_space=pltpu.VMEM)
        anywhere = pl.BlockSpec(memory_space=pl.ANY)
        S = pltpu.SMEM
        V = pltpu.VMEM
        call = pl.pallas_call(
            lambda *refs: kernel(gx_tiles, gy_tiles, steps, *refs),
            out_shape=out,
            in_specs=[anywhere] * 12,
            out_specs=vmem,
            scratch_shapes=[
                V((2, 9, nz, cx, cy), jnp.bfloat16),
                V((3, nz, cx, cy), f32),
                S((1, steps), f32),
                V((steps, 1, residual.shape[2]), f32),
                S((1,), jnp.int32),
                S((1,), jnp.int32),
                V((1, residual.shape[2]), jnp.int32),
                V((1, residual.shape[2]), jnp.int32),
                S((1, 1, 1), jnp.int32),
                pltpu.SemaphoreType.DMA((12,)),
                V((2, 9, HALO, nz, cy), jnp.bfloat16),
                V((2, 9, HALO, nz, cy), jnp.bfloat16),
                V((2, 3, HALO, nz, cy), f32),
                V((18, wide, nz, 2 * cy), f32),
                V((3, wide, nz, 2 * cy), f32),
                V((2, 9, HALO, nz, cy), jnp.bfloat16),
                V((2, 9, HALO, nz, cy), jnp.bfloat16),
                V((3, HALO, nz, cy), f32),
                V((3, HALO, nz, cy), f32),
                V((cx, nz, cy), f32),
                V((wide, nz, cy), f32),
                V((wide, nz, cy), f32),
                V((2, steps, 6, wide, nz, cy), f32),
                V((2, steps, 3, wide, nz, cy), f32),
                V((steps, 16, 2 * cy), f32),
                V((3, cx, nz, cy), f32),
                V((CORES, HALVES, RING, 3, cx, cy), f32),
                V((HALVES, RING, 3, cx, cy), f32),
                V((HALVES, RING, 3, cx, cy), f32),
                V((RING - 1, HALVES, 3, cx, cy), f32),
                V((HALVES, 3, cx, cy), f32),
                V((3, cx, cy), f32),
                pltpu.SemaphoreType.DMA((17,)),
                pltpu.SemaphoreType.DMA((17,)),
            ],
            compiler_params=pltpu.CompilerParams(collective_id=0, has_side_effects=True),
        )
        sums = call(
            forward_state, adjoint_state, lame, shear, density, wavelet, residual.swapaxes(0, 1),
            source_x, source_y, receiver_x, receiver_y, aperture,
        )
        return sums[0:1], sums[1:2], sums[2:3]

    return jax.shard_map(
        local,
        mesh=mesh,
        in_specs=(
            P("shot", None, None, "gx", "gy"),
            P("shot", None, None, "gx", "gy"),
            P(None, "gx", "gy"),
            P(None, "gx", "gy"),
            P(None, "gx", "gy"),
            P("shot", None),
            P("shot", None, None),
            P("shot"),
            P("shot"),
            P("shot", None),
            P("shot", None),
            P("shot", "gx", "gy"),
        ),
        out_specs=(P("shot", "gx", "gy"), P("shot", "gx", "gy"), P("shot", "gx", "gy")),
        check_vma=False,
    )
```

```python
import jax
import jax.numpy as jnp
from jax import lax
from jax.experimental import pallas as pl
from jax.experimental.pallas import tpu as pltpu
from jax.sharding import PartitionSpec as P

courant = 0.2
HALO = 3
MESH = pl.DeviceIdType.MESH
CORES, RING, HALVES = 2, 4, 2


def kernel(
    gx_tiles, gy_tiles, steps,
    forward_hbm, adjoint_hbm, lame_hbm, shear_hbm, density_hbm,
    wavelet_hbm, residual_hbm, source_x_hbm, source_y_hbm, receiver_x_hbm, receiver_y_hbm, aperture_hbm,
    out,
    raw, raw_model, wavelet, residual, source_x, source_y, receiver_x, receiver_y, aperture, fetch,
    edge_low, edge_high, edge_model, field, model, x_low, x_high, m_low, m_high, pack, pack_low, pack_high,
    strain, motion, lifted, term, chunks, got_core, sum_core, got_ring, sum_ring, got_half,
    send, recv,
):
    runs, fields, nz, cx, cy = raw.shape
    fields2 = runs * fields
    wide = cx + 2 * HALO
    sources = (
        lame_hbm, shear_hbm, density_hbm, forward_hbm.at[0], adjoint_hbm.at[0], wavelet_hbm, residual_hbm,
        source_x_hbm, source_y_hbm, receiver_x_hbm, receiver_y_hbm, aperture_hbm,
    )
    targets = (
        raw_model.at[0], raw_model.at[1], raw_model.at[2], raw.at[0], raw.at[1], wavelet, residual,
        source_x, source_y, receiver_x, receiver_y, aperture,
    )
    fetched = [
        pltpu.make_async_copy(source, target, fetch.at[n])
        for n, (source, target) in enumerate(zip(sources, targets))
    ]
    for copy in fetched:
        copy.start()

    gx, gy, shot = lax.axis_index("gx"), lax.axis_index("gy"), lax.axis_index("shot")
    half, ring, core = shot // (RING * CORES), lax.rem(shot // CORES, RING), lax.rem(shot, CORES)
    x_start, y_start = gx * cx, gy * cy

    def there(dx, dy):
        ok = None
        for delta, at, count in ((dx, gx, gx_tiles), (dy, gy, gy_tiles)):
            if delta:
                one = at > 0 if delta < 0 else at < count - 1
                ok = one if ok is None else jnp.logical_and(ok, one)
        return ok

    def tile(dx, dy):
        return {"gx": gx + dx, "gy": gy + dy}

    near = [(dx, dy) for dx in (-1, 0, 1) for dy in (-1, 0, 1) if dx or dy]

    def shot_at(h, q, c):
        return {"shot": (h * RING + q) * CORES + c}

    peers = [shot_at(half, ring, 1 - core)]
    peers += [shot_at(half, lax.rem(ring + d, RING), core) for d in range(1, RING)]
    peers += [shot_at(1 - half, ring, core)]

    barrier = pltpu.get_barrier_semaphore()
    for peer in peers:
        pl.semaphore_signal(barrier, inc=1, device_id=peer, device_id_type=MESH)
    for dx, dy in near:
        @pl.when(there(dx, dy))
        def _():
            pl.semaphore_signal(barrier, inc=1, device_id=tile(dx, dy), device_id_type=MESH)

    messages = []

    def message(dx, dy, source, target):
        n = len(messages)
        messages.append((dx, dy, pltpu.make_async_remote_copy(
            src_ref=source, dst_ref=target, send_sem=send.at[n], recv_sem=recv.at[n],
            device_id=tile(dx, dy), device_id_type=MESH)))

    for dx in (-1, 1):
        message(dx, 0, edge_model.at[0 if dx < 0 else 1], m_high if dx < 0 else m_low)
    for dx in (-1, 0, 1):
        for dy in (-1, 1):
            side = pack_high if dy < 0 else pack_low
            if dx == 0:
                message(dx, dy, pack, side.at[pl.ds(HALO, cx)])
            else:
                row = HALO + cx if dx < 0 else 0
                source = pack.at[pl.ds(0 if dx < 0 else cx - HALO, HALO)]
                message(dx, dy, source, side.at[pl.ds(row, HALO)])
    shared = len(messages)
    for run in range(runs):
        for dx in (-1, 1):
            side = x_high if dx < 0 else x_low
            message(dx, 0, (edge_low if dx < 0 else edge_high).at[run], side.at[run])

    def issue(numbers):
        for n in numbers:
            dx, dy, copy = messages[n]
            @pl.when(there(dx, dy))
            def _():
                copy.start()

    for n in range(3):
        fetched[n].wait()
    for f in range(3):
        value = raw_model[f]
        if f == 2:
            value = courant * (1.0 / value)
        turned = jnp.swapaxes(value, 0, 1)
        model[f, HALO : HALO + cx, :, 0:cy] = turned
        edge_model[0, f] = turned[:HALO]
        edge_model[1, f] = turned[cx - HALO :]
    for run in range(runs):
        fetched[3 + run].wait()

        def turn(f, carry):
            turned = jnp.swapaxes(raw[run, f].astype(jnp.float32), 0, 1)
            field[fields * run + f, HALO : HALO + cx, :, 0:cy] = turned
            edge_low[run, f] = turned[:HALO].astype(jnp.bfloat16)
            edge_high[run, f] = turned[cx - HALO :].astype(jnp.bfloat16)
            return carry

        lax.fori_loop(0, fields, turn, 0)
        if run == 0:
            along_x = jnp.minimum(gx, 1) + jnp.minimum(gx_tiles - 1 - gx, 1) + 1
            along_y = jnp.minimum(gy, 1) + jnp.minimum(gy_tiles - 1 - gy, 1) + 1
            pl.semaphore_wait(barrier, along_x * along_y - 1 + len(peers))
            issue((0, 1, shared, shared + 1))

    def loop(low, high, *bodies):
        def body(i, carry):
            for one in bodies:
                one(i)
            return carry
        lax.fori_loop(low, high, body, 0)

    lane = lax.broadcasted_iota(jnp.int32, (nz, cy), 1)

    def pack_row(x):
        total = jnp.zeros((nz, cy), jnp.float32)
        for f in range(fields2 + 3):
            value = (field[f, x + HALO] if f < fields2 else model[f - fields2, x + HALO])[:, 0:cy]
            moved = pltpu.roll(value, 6 * f + 3, axis=1)
            total = jnp.where((lane >= 6 * f) & (lane < 6 * f + 6), moved, total)
        pack[x] = total

    loop(0, cx // 2, pack_row, lambda x: pack_row(x + cx // 2))
    issue((4, 5, 2, 3, 6, 7, shared + 2, shared + 3))

    def blank(dx, dy, ref):
        @pl.when(jnp.logical_not(there(dx, dy)))
        def _():
            ref[...] = jnp.zeros(ref.shape, ref.dtype)

    for dx, side, model_side in ((-1, x_low, m_low), (1, x_high, m_high)):
        blank(dx, 0, side)
        blank(dx, 0, model_side)
    for dx in (-1, 0, 1):
        for dy, side in ((-1, pack_low), (1, pack_high)):
            row, count = {-1: (0, HALO), 0: (HALO, cx), 1: (HALO + cx, HALO)}[dx]
            blank(dx, dy, side.at[pl.ds(row, count)])

    for copy in fetched[5:]:
        copy.wait()

    lanes2 = lax.broadcasted_iota(jnp.int32, (nz, 2 * cy), 1)
    depth = lax.broadcasted_iota(jnp.int32, (nz, 2 * cy), 0)
    column = jnp.where(lanes2 < cy + cy // 2, lanes2, lanes2 - 2 * cy) + y_start

    receivers = receiver_x.shape[1]
    rows = lax.broadcasted_iota(jnp.int32, (16, receivers), 0) + (x_start - HALO)
    hit_x = rows == receiver_x[...]
    cells = lax.broadcasted_iota(jnp.int32, (2 * cy, receivers), 0)
    cells = jnp.where(cells < cy + cy // 2, cells, cells - 2 * cy) + y_start
    hit_y = jnp.where(cells == receiver_y[...], 1.0, 0.0).astype(jnp.float32)
    for n in range(steps):
        picked = jnp.where(hit_x, residual[n], 0.0)
        lifted[n] = lax.dot_general(
            picked, hit_y, (((1,), (1,)), ((), ())),
            precision=lax.Precision.HIGHEST, preferred_element_type=jnp.float32)

    def wait_recv(n):
        dx, dy, copy = messages[n]
        @pl.when(there(-dx, -dy))
        def _():
            copy.wait_recv()

    lane6 = lax.rem(lane, 6)
    at_edge = (lane < HALO) | (lane >= cy - HALO)

    def unpack_row(x):
        both = jnp.where(lane6 < 3, pack_low[x], pack_high[x])
        for f in range(fields2 + 3):
            moved = pltpu.roll(both, (cy - HALO - 6 * f) % cy, axis=1)
            moved = jnp.where(at_edge, moved, 0.0)
            if f < fields2:
                field[f, x, :, cy : 2 * cy] = moved
            else:
                model[f - fields2, x, :, cy : 2 * cy] = moved

    def x_halo(run):
        def body(f):
            for x in range(HALO):
                field[9 * run + f, x, :, 0:cy] = x_low[run, f, x].astype(jnp.float32)
                field[9 * run + f, HALO + cx + x, :, 0:cy] = x_high[run, f, x].astype(jnp.float32)
        loop(0, 9, body)

    first_z, last_z = depth == 0, depth == nz - 1

    def y_next(v):
        return pltpu.roll(v, 2 * cy - 1, axis=1)

    def y_back(v):
        return pltpu.roll(v, 1, axis=1)

    def z_next(v):
        return jnp.where(last_z, 0.0, pltpu.roll(v, nz - 1, axis=0))

    def z_back(v):
        return jnp.where(first_z, 0.0, pltpu.roll(v, 1, axis=0))

    pulse_at = jnp.where((depth == 2) & (column == source_y[0]), 1.0, 0.0).astype(jnp.float32)
    lift_at = depth == 1

    def velocity(run, n, j):
        vx, vy, vz, sxx, syy, szz, sxy, sxz, syz = range(9 * run, 9 * run + 9)
        k = j + 1
        b0, b1 = model[2, j], model[2, k]
        xy0, xy1, xz0, xz1 = field[sxy, j], field[sxy, k], field[sxz, j], field[sxz, k]
        yy, zz, yz = field[syy, k], field[szz, k], field[syz, k]
        gain_x = b0 * ((field[sxx, k] - field[sxx, j]) + (xy0 - y_back(xy0)) + (xz0 - z_back(xz0)))
        gain_y = b1 * ((xy1 - xy0) + (y_next(yy) - yy) + (yz - z_back(yz)))
        gain_z = b1 * ((xz1 - xz0) + (yz - y_back(yz)) + (z_next(zz) - zz))
        new_x, new_y = field[vx, j] + gain_x, field[vy, k] + gain_y
        new_z = field[vz, k] + gain_z
        if run == 1:
            row = lifted[steps - 1 - n, pl.ds(k, 1), :]
            new_z = new_z + jnp.where(lift_at, row, 0.0)
        field[vx, j], field[vy, k], field[vz, k] = new_x, new_y, new_z
        if run == 0:
            saved = (gain_x * (1.0 / courant), gain_y * (1.0 / courant), gain_z * (1.0 / courant))
        else:
            saved = (new_x, new_y, new_z)
        motion[run, n, 0, j] = saved[0][:, 0:cy]
        motion[run, n, 1, k] = saved[1][:, 0:cy]
        motion[run, n, 2, k] = saved[2][:, 0:cy]

    def stress(run, n, k):
        vx, vy, vz, sxx, syy, szz, sxy, sxz, syz = range(9 * run, 9 * run + 9)
        x0, y0, z0 = field[vx, k], field[vy, k], field[vz, k]
        e = (
            x0 - field[vx, k - 1],
            y0 - y_back(y0),
            z0 - z_back(z0),
            (y_next(x0) - x0) + (field[vy, k + 1] - y0),
            (z_next(x0) - x0) + (field[vz, k + 1] - z0),
            (z_next(y0) - y0) + (y_next(z0) - z0),
        )
        for c in range(6):
            strain[run, n, c, k] = e[c][:, 0:cy]
        if n < steps - 1:
            scaled = courant * model[1, k]
            bulk = courant * model[0, k] * (e[0] + e[1] + e[2])
            if run == 0:
                amount = jnp.where(x_start + k - HALO == source_x[0], wavelet[0, n], 0.0)
                bulk = bulk + amount * pulse_at
            for c in range(3):
                field[sxx + c, k] = field[sxx + c, k] + (bulk + 2.0 * scaled * e[c])
            for c in range(3, 6):
                field[sxx + c, k] = field[sxx + c, k] + scaled * e[c]

    wait_recv(4)
    wait_recv(5)
    loop(0, cx // 2, lambda x: unpack_row(x + HALO), lambda x: unpack_row(x + HALO + cx // 2))
    for n in range(steps):
        loop(HALO + n, cx + HALO - 1 - n, lambda j: velocity(0, n, j), lambda j: velocity(1, n, j))
        loop(HALO + 1 + n, cx + HALO - 1 - n, lambda k: stress(0, n, k), lambda k: stress(1, n, k))

    for n in (0, 1, 2, 3, 6, 7):
        wait_recv(n)
    for f in range(3):
        for x in range(HALO):
            model[f, x, :, 0:cy] = m_low[f, x]
            model[f, HALO + cx + x, :, 0:cy] = m_high[f, x]
    loop(0, HALO, unpack_row, lambda x: unpack_row(x + HALO + cx))
    for run in range(runs):
        wait_recv(shared + 2 * run)
        wait_recv(shared + 2 * run + 1)
        x_halo(run)
        for n in range(steps):
            high = cx + HALO - 1 - n
            loop(0, HALO, lambda i: velocity(run, n, i + n), lambda i: velocity(run, n, i + high))
            loop(0, HALO, lambda i: stress(run, n, i + n + 1), lambda i: stress(run, n, i + high))

    factor = (-courant / (HALVES * RING * CORES)) * aperture[0, 0, 0].astype(jnp.float32)

    def image(x):
        k = x + HALO
        first = second = third = jnp.zeros((nz, cy), jnp.float32)
        for m in range(steps):
            n = steps - 1 - m
            e = [strain[0, n, c, k] for c in range(6)]
            f = [strain[1, m, c, k] for c in range(6)]
            first = first + (e[0] + e[1] + e[2]) * (f[0] + f[1] + f[2])
            second = second + 2.0 * (e[0] * f[0] + e[1] * f[1] + e[2] * f[2])
            second = second + e[3] * f[3] + e[4] * f[4] + e[5] * f[5]
            for c in range(3):
                third = third + motion[0, n, c, k] * motion[1, m, c, k]
        term[0, x], term[1, x], term[2, x] = factor * first, factor * second, factor * third

    loop(0, cx // 2, image, lambda x: image(x + cx // 2))

    for t in range(3):
        turned = jnp.swapaxes(term[t], 0, 1)
        for z in range(nz):
            chunks[z % CORES, z // (CORES * RING), (z // CORES) % RING, t] = turned[z]

    count = len(messages)
    last = []

    def push(source, target, peer):
        n = count + len(last)
        copy = pltpu.make_async_remote_copy(
            src_ref=source, dst_ref=target, send_sem=send.at[n], recv_sem=recv.at[n],
            device_id=peer, device_id_type=MESH)
        copy.start()
        last.append(copy)
        return copy

    groups = (1 - half, half)
    cores = [push(chunks.at[1 - core, g], got_core.at[n], peers[0]) for n, g in enumerate(groups)]
    rings = []
    for n, g in enumerate(groups):
        cores[n].wait_recv()
        sum_core[n] = chunks[core, g] + got_core[n]
        rings.append([
            push(sum_core.at[n, lax.rem(ring + d, RING)], got_ring.at[n, d - 1], peers[d])
            for d in range(1, RING)
        ])
    for n in range(HALVES):
        total = sum_core[n, ring]
        for d in range(1, RING):
            rings[n][d - 1].wait_recv()
            total = total + got_ring[n, d - 1]
        if n == 0:
            sum_ring[...] = total
            across = push(sum_ring, got_half, peers[RING])
    across.wait_recv()
    out[...] = total + got_half[...]
    for copy in last:
        copy.wait_send()
    for dx, dy, copy in messages:
        @pl.when(there(dx, dy))
        def _():
            copy.wait_send()


def solution(mesh):
    gx_tiles, gy_tiles = mesh.shape["gx"], mesh.shape["gy"]

    def local(
        forward_state, adjoint_state, lame, shear, density, wavelet, residual,
        source_x, source_y, receiver_x, receiver_y, aperture,
    ):
        nz, cx, cy = lame.shape
        steps = wavelet.shape[1]
        wide = cx + 2 * HALO
        f32 = jnp.float32
        out = jax.ShapeDtypeStruct((3, cx, cy), f32)
        vmem = pl.BlockSpec(memory_space=pltpu.VMEM)
        anywhere = pl.BlockSpec(memory_space=pl.ANY)
        S = pltpu.SMEM
        V = pltpu.VMEM
        call = pl.pallas_call(
            lambda *refs: kernel(gx_tiles, gy_tiles, steps, *refs),
            out_shape=out,
            in_specs=[anywhere] * 12,
            out_specs=vmem,
            scratch_shapes=[
                V((2, 9, nz, cx, cy), jnp.bfloat16),
                V((3, nz, cx, cy), f32),
                S((1, steps), f32),
                V((steps, 1, residual.shape[2]), f32),
                S((1,), jnp.int32),
                S((1,), jnp.int32),
                V((1, residual.shape[2]), jnp.int32),
                V((1, residual.shape[2]), jnp.int32),
                S((1, 1, 1), jnp.int32),
                pltpu.SemaphoreType.DMA((12,)),
                V((2, 9, HALO, nz, cy), jnp.bfloat16),
                V((2, 9, HALO, nz, cy), jnp.bfloat16),
                V((2, 3, HALO, nz, cy), f32),
                V((18, wide, nz, 2 * cy), f32),
                V((3, wide, nz, 2 * cy), f32),
                V((2, 9, HALO, nz, cy), jnp.bfloat16),
                V((2, 9, HALO, nz, cy), jnp.bfloat16),
                V((3, HALO, nz, cy), f32),
                V((3, HALO, nz, cy), f32),
                V((cx, nz, cy), f32),
                V((wide, nz, cy), f32),
                V((wide, nz, cy), f32),
                V((2, steps, 6, wide, nz, cy), f32),
                V((2, steps, 3, wide, nz, cy), f32),
                V((steps, 16, 2 * cy), f32),
                V((3, cx, nz, cy), f32),
                V((CORES, HALVES, RING, 3, cx, cy), f32),
                V((HALVES, RING, 3, cx, cy), f32),
                V((HALVES, RING, 3, cx, cy), f32),
                V((HALVES, RING - 1, 3, cx, cy), f32),
                V((3, cx, cy), f32),
                V((3, cx, cy), f32),
                pltpu.SemaphoreType.DMA((21,)),
                pltpu.SemaphoreType.DMA((21,)),
            ],
            compiler_params=pltpu.CompilerParams(collective_id=0, has_side_effects=True),
        )
        sums = call(
            forward_state, adjoint_state, lame, shear, density, wavelet, residual.swapaxes(0, 1),
            source_x, source_y, receiver_x, receiver_y, aperture,
        )
        return sums[0:1], sums[1:2], sums[2:3]

    return jax.shard_map(
        local,
        mesh=mesh,
        in_specs=(
            P("shot", None, None, "gx", "gy"),
            P("shot", None, None, "gx", "gy"),
            P(None, "gx", "gy"),
            P(None, "gx", "gy"),
            P(None, "gx", "gy"),
            P("shot", None),
            P("shot", None, None),
            P("shot"),
            P("shot"),
            P("shot", None),
            P("shot", None),
            P("shot", "gx", "gy"),
        ),
        out_specs=(P("shot", "gx", "gy"), P("shot", "gx", "gy"), P("shot", "gx", "gy")),
        check_vma=False,
    )
```

```python
import jax
import jax.numpy as jnp
from jax import lax
from jax.experimental import pallas as pl
from jax.experimental.pallas import tpu as pltpu
from jax.sharding import PartitionSpec as P

courant = 0.2
HALO = 3
MESH = pl.DeviceIdType.MESH
CORES, RING, HALVES = 2, 4, 2


def kernel(
    gx_tiles, gy_tiles, steps,
    forward_hbm, adjoint_hbm, lame_hbm, shear_hbm, density_hbm,
    wavelet_hbm, residual_hbm, source_x_hbm, source_y_hbm, receiver_x_hbm, receiver_y_hbm, aperture_hbm,
    out,
    raw, raw_model, wavelet, residual, source_x, source_y, receiver_x, receiver_y, aperture, fetch,
    edge_low, edge_high, edge_model, field, model, x_low, x_high, m_low, m_high, pack, pack_low, pack_high,
    strain, motion, lifted, term, chunks, got_core, sum_core, got_ring, sum_ring, got_half,
    send, recv,
):
    runs, fields, nz, cx, cy = raw.shape
    fields2 = runs * fields
    wide = cx + 2 * HALO
    sources = (
        lame_hbm, shear_hbm, density_hbm, forward_hbm.at[0], adjoint_hbm.at[0], wavelet_hbm, residual_hbm,
        source_x_hbm, source_y_hbm, receiver_x_hbm, receiver_y_hbm, aperture_hbm,
    )
    targets = (
        raw_model.at[0], raw_model.at[1], raw_model.at[2], raw.at[0], raw.at[1], wavelet, residual,
        source_x, source_y, receiver_x, receiver_y, aperture,
    )
    fetched = [
        pltpu.make_async_copy(source, target, fetch.at[n])
        for n, (source, target) in enumerate(zip(sources, targets))
    ]
    for copy in fetched:
        copy.start()

    gx, gy, shot = lax.axis_index("gx"), lax.axis_index("gy"), lax.axis_index("shot")
    half, ring, core = shot // (RING * CORES), lax.rem(shot // CORES, RING), lax.rem(shot, CORES)
    x_start, y_start = gx * cx, gy * cy

    def there(dx, dy):
        ok = None
        for delta, at, count in ((dx, gx, gx_tiles), (dy, gy, gy_tiles)):
            if delta:
                one = at > 0 if delta < 0 else at < count - 1
                ok = one if ok is None else jnp.logical_and(ok, one)
        return ok

    def tile(dx, dy):
        return {"gx": gx + dx, "gy": gy + dy}

    near = [(dx, dy) for dx in (-1, 0, 1) for dy in (-1, 0, 1) if dx or dy]

    def shot_at(h, q, c):
        return {"shot": (h * RING + q) * CORES + c}

    peers = [shot_at(half, ring, 1 - core)]
    peers += [shot_at(half, lax.rem(ring + d, RING), core) for d in range(1, RING)]
    peers += [shot_at(1 - half, ring, core)]

    barrier = pltpu.get_barrier_semaphore()
    for peer in peers:
        pl.semaphore_signal(barrier, inc=1, device_id=peer, device_id_type=MESH)
    for dx, dy in near:
        @pl.when(there(dx, dy))
        def _():
            pl.semaphore_signal(barrier, inc=1, device_id=tile(dx, dy), device_id_type=MESH)

    messages = []

    def message(dx, dy, source, target):
        n = len(messages)
        messages.append((dx, dy, pltpu.make_async_remote_copy(
            src_ref=source, dst_ref=target, send_sem=send.at[n], recv_sem=recv.at[n],
            device_id=tile(dx, dy), device_id_type=MESH)))

    for dx in (-1, 1):
        message(dx, 0, edge_model.at[0 if dx < 0 else 1], m_high if dx < 0 else m_low)
    for dx in (-1, 0, 1):
        for dy in (-1, 1):
            side = pack_high if dy < 0 else pack_low
            if dx == 0:
                message(dx, dy, pack, side.at[pl.ds(HALO, cx)])
            else:
                row = HALO + cx if dx < 0 else 0
                source = pack.at[pl.ds(0 if dx < 0 else cx - HALO, HALO)]
                message(dx, dy, source, side.at[pl.ds(row, HALO)])
    shared = len(messages)
    for run in range(runs):
        for dx in (-1, 1):
            side = x_high if dx < 0 else x_low
            message(dx, 0, (edge_low if dx < 0 else edge_high).at[run], side.at[run])

    def issue(numbers):
        for n in numbers:
            dx, dy, copy = messages[n]
            @pl.when(there(dx, dy))
            def _():
                copy.start()

    for n in range(3):
        fetched[n].wait()
    for f in range(3):
        value = raw_model[f]
        if f == 2:
            value = courant * (1.0 / value)
        turned = jnp.swapaxes(value, 0, 1)
        model[f, HALO : HALO + cx, :, 0:cy] = turned
        edge_model[0, f] = turned[:HALO]
        edge_model[1, f] = turned[cx - HALO :]
    for run in range(runs):
        fetched[3 + run].wait()

        def turn(f, carry):
            turned = jnp.swapaxes(raw[run, f].astype(jnp.float32), 0, 1)
            field[fields * run + f, HALO : HALO + cx, :, 0:cy] = turned
            edge_low[run, f] = turned[:HALO].astype(jnp.bfloat16)
            edge_high[run, f] = turned[cx - HALO :].astype(jnp.bfloat16)
            return carry

        lax.fori_loop(0, fields, turn, 0)
        if run == 0:
            along_x = jnp.minimum(gx, 1) + jnp.minimum(gx_tiles - 1 - gx, 1) + 1
            along_y = jnp.minimum(gy, 1) + jnp.minimum(gy_tiles - 1 - gy, 1) + 1
            pl.semaphore_wait(barrier, along_x * along_y - 1 + len(peers))
            issue((0, 1, shared, shared + 1))

    def loop(low, high, *bodies):
        def body(i, carry):
            for one in bodies:
                one(i)
            return carry
        lax.fori_loop(low, high, body, 0)

    lane = lax.broadcasted_iota(jnp.int32, (nz, cy), 1)

    def pack_row(x):
        total = jnp.zeros((nz, cy), jnp.float32)
        for f in range(fields2 + 3):
            value = (field[f, x + HALO] if f < fields2 else model[f - fields2, x + HALO])[:, 0:cy]
            moved = pltpu.roll(value, 6 * f + 3, axis=1)
            total = jnp.where((lane >= 6 * f) & (lane < 6 * f + 6), moved, total)
        pack[x] = total

    loop(0, cx // 2, pack_row, lambda x: pack_row(x + cx // 2))
    issue((4, 5, 2, 3, 6, 7, shared + 2, shared + 3))

    def blank(dx, dy, ref):
        @pl.when(jnp.logical_not(there(dx, dy)))
        def _():
            ref[...] = jnp.zeros(ref.shape, ref.dtype)

    for dx, side, model_side in ((-1, x_low, m_low), (1, x_high, m_high)):
        blank(dx, 0, side)
        blank(dx, 0, model_side)
    for dx in (-1, 0, 1):
        for dy, side in ((-1, pack_low), (1, pack_high)):
            row, count = {-1: (0, HALO), 0: (HALO, cx), 1: (HALO + cx, HALO)}[dx]
            blank(dx, dy, side.at[pl.ds(row, count)])

    for copy in fetched[5:]:
        copy.wait()

    lanes2 = lax.broadcasted_iota(jnp.int32, (nz, 2 * cy), 1)
    depth = lax.broadcasted_iota(jnp.int32, (nz, 2 * cy), 0)
    column = jnp.where(lanes2 < cy + cy // 2, lanes2, lanes2 - 2 * cy) + y_start

    receivers = receiver_x.shape[1]
    rows = lax.broadcasted_iota(jnp.int32, (16, receivers), 0) + (x_start - HALO)
    hit_x = rows == receiver_x[...]
    cells = lax.broadcasted_iota(jnp.int32, (2 * cy, receivers), 0)
    cells = jnp.where(cells < cy + cy // 2, cells, cells - 2 * cy) + y_start
    hit_y = jnp.where(cells == receiver_y[...], 1.0, 0.0).astype(jnp.float32)
    for n in range(steps):
        picked = jnp.where(hit_x, residual[n], 0.0)
        lifted[n] = lax.dot_general(
            picked, hit_y, (((1,), (1,)), ((), ())),
            precision=lax.Precision.HIGHEST, preferred_element_type=jnp.float32)

    def wait_recv(n):
        dx, dy, copy = messages[n]
        @pl.when(there(-dx, -dy))
        def _():
            copy.wait_recv()

    lane6 = lax.rem(lane, 6)
    at_edge = (lane < HALO) | (lane >= cy - HALO)

    def unpack_row(x):
        both = jnp.where(lane6 < 3, pack_low[x], pack_high[x])
        for f in range(fields2 + 3):
            moved = pltpu.roll(both, (cy - HALO - 6 * f) % cy, axis=1)
            moved = jnp.where(at_edge, moved, 0.0)
            if f < fields2:
                field[f, x, :, cy : 2 * cy] = moved
            else:
                model[f - fields2, x, :, cy : 2 * cy] = moved

    def x_halo(run):
        def body(f):
            for x in range(HALO):
                field[9 * run + f, x, :, 0:cy] = x_low[run, f, x].astype(jnp.float32)
                field[9 * run + f, HALO + cx + x, :, 0:cy] = x_high[run, f, x].astype(jnp.float32)
        loop(0, 9, body)

    first_z, last_z = depth == 0, depth == nz - 1

    def y_next(v):
        return pltpu.roll(v, 2 * cy - 1, axis=1)

    def y_back(v):
        return pltpu.roll(v, 1, axis=1)

    def z_next(v):
        return jnp.where(last_z, 0.0, pltpu.roll(v, nz - 1, axis=0))

    def z_back(v):
        return jnp.where(first_z, 0.0, pltpu.roll(v, 1, axis=0))

    pulse_at = jnp.where((depth == 2) & (column == source_y[0]), 1.0, 0.0).astype(jnp.float32)
    lift_at = depth == 1

    def velocity(run, n, j):
        vx, vy, vz, sxx, syy, szz, sxy, sxz, syz = range(9 * run, 9 * run + 9)
        k = j + 1
        b0, b1 = model[2, j], model[2, k]
        xy0, xy1, xz0, xz1 = field[sxy, j], field[sxy, k], field[sxz, j], field[sxz, k]
        yy, zz, yz = field[syy, k], field[szz, k], field[syz, k]
        gain_x = b0 * ((field[sxx, k] - field[sxx, j]) + (xy0 - y_back(xy0)) + (xz0 - z_back(xz0)))
        gain_y = b1 * ((xy1 - xy0) + (y_next(yy) - yy) + (yz - z_back(yz)))
        gain_z = b1 * ((xz1 - xz0) + (yz - y_back(yz)) + (z_next(zz) - zz))
        new_x, new_y = field[vx, j] + gain_x, field[vy, k] + gain_y
        new_z = field[vz, k] + gain_z
        if run == 1:
            row = lifted[steps - 1 - n, pl.ds(k, 1), :]
            new_z = new_z + jnp.where(lift_at, row, 0.0)
        field[vx, j], field[vy, k], field[vz, k] = new_x, new_y, new_z
        if run == 0:
            saved = (gain_x * (1.0 / courant), gain_y * (1.0 / courant), gain_z * (1.0 / courant))
        else:
            saved = (new_x, new_y, new_z)
        motion[run, n, 0, j] = saved[0][:, 0:cy]
        motion[run, n, 1, k] = saved[1][:, 0:cy]
        motion[run, n, 2, k] = saved[2][:, 0:cy]

    def stress(run, n, k):
        vx, vy, vz, sxx, syy, szz, sxy, sxz, syz = range(9 * run, 9 * run + 9)
        x0, y0, z0 = field[vx, k], field[vy, k], field[vz, k]
        e = (
            x0 - field[vx, k - 1],
            y0 - y_back(y0),
            z0 - z_back(z0),
            (y_next(x0) - x0) + (field[vy, k + 1] - y0),
            (z_next(x0) - x0) + (field[vz, k + 1] - z0),
            (z_next(y0) - y0) + (y_next(z0) - z0),
        )
        for c in range(6):
            strain[run, n, c, k] = e[c][:, 0:cy]
        if n < steps - 1:
            scaled = courant * model[1, k]
            bulk = courant * model[0, k] * (e[0] + e[1] + e[2])
            if run == 0:
                amount = jnp.where(x_start + k - HALO == source_x[0], wavelet[0, n], 0.0)
                bulk = bulk + amount * pulse_at
            for c in range(3):
                field[sxx + c, k] = field[sxx + c, k] + (bulk + 2.0 * scaled * e[c])
            for c in range(3, 6):
                field[sxx + c, k] = field[sxx + c, k] + scaled * e[c]

    wait_recv(4)
    wait_recv(5)
    loop(0, cx // 2, lambda x: unpack_row(x + HALO), lambda x: unpack_row(x + HALO + cx // 2))
    for n in range(steps):
        loop(HALO + n, cx + HALO - 1 - n, lambda j: velocity(0, n, j), lambda j: velocity(1, n, j))
        loop(HALO + 1 + n, cx + HALO - 1 - n, lambda k: stress(0, n, k), lambda k: stress(1, n, k))

    for n in (0, 1, 2, 3, 6, 7):
        wait_recv(n)
    for f in range(3):
        for x in range(HALO):
            model[f, x, :, 0:cy] = m_low[f, x]
            model[f, HALO + cx + x, :, 0:cy] = m_high[f, x]
    loop(0, HALO, unpack_row, lambda x: unpack_row(x + HALO + cx))
    for run in range(runs):
        wait_recv(shared + 2 * run)
        wait_recv(shared + 2 * run + 1)
        x_halo(run)
    for n in range(steps):
        high = cx + HALO - 1 - n
        loop(0, HALO, *[
            lambda i, run=run, row=row: velocity(run, n, i + row) for run in range(runs) for row in (n, high)
        ])
        loop(0, HALO, *[
            lambda i, run=run, row=row: stress(run, n, i + row) for run in range(runs) for row in (n + 1, high)
        ])

    factor = (-courant / (HALVES * RING * CORES)) * aperture[0, 0, 0].astype(jnp.float32)

    def image(x):
        k = x + HALO
        first = second = third = jnp.zeros((nz, cy), jnp.float32)
        for m in range(steps):
            n = steps - 1 - m
            e = [strain[0, n, c, k] for c in range(6)]
            f = [strain[1, m, c, k] for c in range(6)]
            first = first + (e[0] + e[1] + e[2]) * (f[0] + f[1] + f[2])
            second = second + 2.0 * (e[0] * f[0] + e[1] * f[1] + e[2] * f[2])
            second = second + e[3] * f[3] + e[4] * f[4] + e[5] * f[5]
            for c in range(3):
                third = third + motion[0, n, c, k] * motion[1, m, c, k]
        term[0, x], term[1, x], term[2, x] = factor * first, factor * second, factor * third

    loop(0, cx // 2, image, lambda x: image(x + cx // 2))

    for t in range(3):
        turned = jnp.swapaxes(term[t], 0, 1)
        for z in range(nz):
            chunks[z % CORES, z // (CORES * RING), (z // CORES) % RING, t] = turned[z]

    count = len(messages)
    last = []

    def push(source, target, peer):
        n = count + len(last)
        copy = pltpu.make_async_remote_copy(
            src_ref=source, dst_ref=target, send_sem=send.at[n], recv_sem=recv.at[n],
            device_id=peer, device_id_type=MESH)
        copy.start()
        last.append(copy)
        return copy

    groups = (1 - half, half)
    cores = [push(chunks.at[1 - core, g], got_core.at[n], peers[0]) for n, g in enumerate(groups)]
    rings = []
    for n, g in enumerate(groups):
        cores[n].wait_recv()
        sum_core[n] = chunks[core, g] + got_core[n]
        rings.append([
            push(sum_core.at[n, lax.rem(ring + d, RING)], got_ring.at[n, d - 1], peers[d])
            for d in range(1, RING)
        ])
    for n in range(HALVES):
        total = sum_core[n, ring]
        for d in range(1, RING):
            rings[n][d - 1].wait_recv()
            total = total + got_ring[n, d - 1]
        if n == 0:
            sum_ring[...] = total
            across = push(sum_ring, got_half, peers[RING])
    across.wait_recv()
    out[...] = total + got_half[...]
    for copy in last:
        copy.wait_send()
    for dx, dy, copy in messages:
        @pl.when(there(dx, dy))
        def _():
            copy.wait_send()


def solution(mesh):
    gx_tiles, gy_tiles = mesh.shape["gx"], mesh.shape["gy"]

    def local(
        forward_state, adjoint_state, lame, shear, density, wavelet, residual,
        source_x, source_y, receiver_x, receiver_y, aperture,
    ):
        nz, cx, cy = lame.shape
        steps = wavelet.shape[1]
        wide = cx + 2 * HALO
        f32 = jnp.float32
        out = jax.ShapeDtypeStruct((3, cx, cy), f32)
        vmem = pl.BlockSpec(memory_space=pltpu.VMEM)
        anywhere = pl.BlockSpec(memory_space=pl.ANY)
        S = pltpu.SMEM
        V = pltpu.VMEM
        call = pl.pallas_call(
            lambda *refs: kernel(gx_tiles, gy_tiles, steps, *refs),
            out_shape=out,
            in_specs=[anywhere] * 12,
            out_specs=vmem,
            scratch_shapes=[
                V((2, 9, nz, cx, cy), jnp.bfloat16),
                V((3, nz, cx, cy), f32),
                S((1, steps), f32),
                V((steps, 1, residual.shape[2]), f32),
                S((1,), jnp.int32),
                S((1,), jnp.int32),
                V((1, residual.shape[2]), jnp.int32),
                V((1, residual.shape[2]), jnp.int32),
                S((1, 1, 1), jnp.int32),
                pltpu.SemaphoreType.DMA((12,)),
                V((2, 9, HALO, nz, cy), jnp.bfloat16),
                V((2, 9, HALO, nz, cy), jnp.bfloat16),
                V((2, 3, HALO, nz, cy), f32),
                V((18, wide, nz, 2 * cy), f32),
                V((3, wide, nz, 2 * cy), f32),
                V((2, 9, HALO, nz, cy), jnp.bfloat16),
                V((2, 9, HALO, nz, cy), jnp.bfloat16),
                V((3, HALO, nz, cy), f32),
                V((3, HALO, nz, cy), f32),
                V((cx, nz, cy), f32),
                V((wide, nz, cy), f32),
                V((wide, nz, cy), f32),
                V((2, steps, 6, wide, nz, cy), f32),
                V((2, steps, 3, wide, nz, cy), f32),
                V((steps, 16, 2 * cy), f32),
                V((3, cx, nz, cy), f32),
                V((CORES, HALVES, RING, 3, cx, cy), f32),
                V((HALVES, RING, 3, cx, cy), f32),
                V((HALVES, RING, 3, cx, cy), f32),
                V((HALVES, RING - 1, 3, cx, cy), f32),
                V((3, cx, cy), f32),
                V((3, cx, cy), f32),
                pltpu.SemaphoreType.DMA((21,)),
                pltpu.SemaphoreType.DMA((21,)),
            ],
            compiler_params=pltpu.CompilerParams(collective_id=0, has_side_effects=True),
        )
        sums = call(
            forward_state, adjoint_state, lame, shear, density, wavelet, residual.swapaxes(0, 1),
            source_x, source_y, receiver_x, receiver_y, aperture,
        )
        return sums[0:1], sums[1:2], sums[2:3]

    return jax.shard_map(
        local,
        mesh=mesh,
        in_specs=(
            P("shot", None, None, "gx", "gy"),
            P("shot", None, None, "gx", "gy"),
            P(None, "gx", "gy"),
            P(None, "gx", "gy"),
            P(None, "gx", "gy"),
            P("shot", None),
            P("shot", None, None),
            P("shot"),
            P("shot"),
            P("shot", None),
            P("shot", None),
            P("shot", "gx", "gy"),
        ),
        out_specs=(P("shot", "gx", "gy"), P("shot", "gx", "gy"), P("shot", "gx", "gy")),
        check_vma=False,
    )
```
